32 devices in a mesh: dp: 4 (over z), ctx: 2 (over y), tp: 4 (over x, core).
Axes of the slice: x: 2, y: 2, z: 4, core: 2. Of those that a mesh axis runs over, the one named last changes fastest.
Arguments:
- tokens: float32 [4, 256, 1024], P('dp', 'ctx'), may hold values from -6 to 6
- cotangent: float32 [4, 256, 1024], P('dp', 'ctx'), may hold values from -6 to 6
- doc_lengths: int32 [4, 8], P('dp'), may hold values from 1 to 64, 256 in all within a row
- norm1_gain: float32 [1024], P(('dp', 'ctx')), may hold values from 0.5 to 1.5
- in_weight: float32 [3, 1024, 1024], P(None, ('dp', 'ctx'), 'tp'), may hold values from -0.1875 to 0.1875
- conv_weight: float32 [3, 1024], P(None, 'tp'), may hold values from -3.5 to 3.5
- out_weight: float32 [1024, 1024], P('tp', ('dp', 'ctx')), may hold values from -0.1875 to 0.1875
- norm2_gain: float32 [1024], P(('dp', 'ctx')), may hold values from 0.5 to 1.5
- gate_up_weight: float32 [2, 1024, 4608], P(None, ('dp', 'ctx'), 'tp'), may hold values from -0.1875 to 0.1875
- down_weight: float32 [4608, 1024], P('tp', ('dp', 'ctx')), may hold values from -0.09375 to 0.09375
- first_norm1: float32 [1024], P(('dp', 'ctx')), may hold values from -6 to 6
- first_in: float32 [3, 1024, 1024], P(None, ('dp', 'ctx'), 'tp'), may hold values from -6 to 6
- first_conv: float32 [3, 1024], P(None, 'tp'), may hold values from -6 to 6
- first_out: float32 [1024, 1024], P('tp', ('dp', 'ctx')), may hold values from -6 to 6
- first_norm2: float32 [1024], P(('dp', 'ctx')), may hold values from -6 to 6
- first_gate_up: float32 [2, 1024, 4608], P(None, ('dp', 'ctx'), 'tp'), may hold values from -6 to 6
- first_down: float32 [4608, 1024], P('tp', ('dp', 'ctx')), may hold values from -6 to 6
- second_norm1: float32 [1024], P(('dp', 'ctx')), may hold values from 1 to 100
- second_in: float32 [3, 1024, 1024], P(None, ('dp', 'ctx'), 'tp'), may hold values from 1 to 100
- second_conv: float32 [3, 1024], P(None, 'tp'), may hold values from 1 to 100
- second_out: float32 [1024, 1024], P('tp', ('dp', 'ctx')), may hold values from 1 to 100
- second_norm2: float32 [1024], P(('dp', 'ctx')), may hold values from 1 to 100
- second_gate_up: float32 [2, 1024, 4608], P(None, ('dp', 'ctx'), 'tp'), may hold values from 1 to 100
- second_down: float32 [4608, 1024], P('tp', ('dp', 'ctx')), may hold values from 1 to 100
Outputs:
- result: float32 [4, 256, 1024], P('dp', 'ctx')
- grad_tokens: float32 [4, 256, 1024], P('dp', 'ctx')
- grad_norm1: float32 [1024], P(('dp', 'ctx'))
- grad_in: float32 [3, 1024, 1024], P(None, ('dp', 'ctx'), 'tp')
- grad_conv: float32 [3, 1024], P(None, 'tp')
- grad_out: float32 [1024, 1024], P('tp', ('dp', 'ctx'))
- grad_norm2: float32 [1024], P(('dp', 'ctx'))
- grad_gate_up: float32 [2, 1024, 4608], P(None, ('dp', 'ctx'), 'tp')
- grad_down: float32 [4608, 1024], P('tp', ('dp', 'ctx'))
- new_norm1: float32 [1024], P(('dp', 'ctx'))
- new_in: float32 [3, 1024, 1024], P(None, ('dp', 'ctx'), 'tp')
- new_conv: float32 [3, 1024], P(None, 'tp')
- new_out: float32 [1024, 1024], P('tp', ('dp', 'ctx'))
- new_norm2: float32 [1024], P(('dp', 'ctx'))
- new_gate_up: float32 [2, 1024, 4608], P(None, ('dp', 'ctx'), 'tp')
- new_down: float32 [4608, 1024], P('tp', ('dp', 'ctx'))
- new_first_norm1: float32 [1024], P(('dp', 'ctx'))
- new_first_in: float32 [3, 1024, 1024], P(None, ('dp', 'ctx'), 'tp')
- new_first_conv: float32 [3, 1024], P(None, 'tp')
- new_first_out: float32 [1024, 1024], P('tp', ('dp', 'ctx'))
- new_first_norm2: float32 [1024], P(('dp', 'ctx'))
- new_first_gate_up: float32 [2, 1024, 4608], P(None, ('dp', 'ctx'), 'tp')
- new_first_down: float32 [4608, 1024], P('tp', ('dp', 'ctx'))
- new_second_norm1: float32 [1024], P(('dp', 'ctx'))
- new_second_in: float32 [3, 1024, 1024], P(None, ('dp', 'ctx'), 'tp')
- new_second_conv: float32 [3, 1024], P(None, 'tp')
- new_second_out: float32 [1024, 1024], P('tp', ('dp', 'ctx'))
- new_second_norm2: float32 [1024], P(('dp', 'ctx'))
- new_second_gate_up: float32 [2, 1024, 4608], P(None, ('dp', 'ctx'), 'tp')
- new_second_down: float32 [4608, 1024], P('tp', ('dp', 'ctx'))
The draws below stay inside these ranges and needn't reach their ends.
Inputs may be any that keep to these rules, and one draw needn't show every extreme that they name: `doc_lengths`: each row holds 8 document lengths that add up to 256; the longest is exactly 64.
All inputs are finite; a program needn't handle non-finite values.
Results may differ from the reference program's by a relative error of at most 0.022.
Values may be sent and summed in bfloat16 or wider, within the bound.
No kernel may reach another device: no remote copies, remote signals or barrier semaphores. Data moves between devices by JAX's collectives and lax.ppermute only.
A program may use at most 128 MiB of HBM per device.

```python
import math
import jax
import jax.numpy as jnp
import numpy as np
from jax import lax

D = 1024
FF = 4608
TAPS = 3
NDOC = 8
STEP = 5
LEN = 256
SEQS = 4
N_TP = 4


def levels(rng, shape, cuts, low, largest):
    def one(dim, shards_of):
        steps = jax.random.uniform(jax.random.fold_in(jax.random.fold_in(rng, 6), dim), (shards_of,), jnp.float32, low / len(cuts), largest / len(cuts))
        return jnp.repeat(jnp.exp(steps), shape[dim] // shards_of).reshape((-1,) + (1,) * (len(shape) - dim - 1))

    gain = one(*cuts[0])
    for cut in cuts[1:]:
        gain = gain * one(*cut)
    return gain


def split_up(number_of, total, reach, lean):
    weights = [(1 << 20) // math.isqrt(grade ** lean) + 1 for grade in range(2, number_of + 1)]
    rest, holding = total - reach - (number_of - 1), [1] * (number_of - 1)
    while rest > 0:
        free = [i for i in range(number_of - 1) if holding[i] < reach]
        whole, budget = sum([weights[i] for i in free]), rest
        for i in free:
            addition = min(reach - holding[i], max(1, budget * weights[i] // whole), rest)
            holding[i] = holding[i] + addition
            rest = rest - addition
    return np.array([reach] + holding)


def uneven(own_key, amount, total, limit, slope):
    if amount == 2:
        one = jax.random.randint(own_key, (), max(1, total - limit), min(limit, total - 1) + 1)
        return jnp.stack([one, total - one])
    tallies = jnp.asarray(split_up(amount, total, limit, slope), jnp.int32)
    twos = (amount - 1) // 2
    donor, taker = tallies[1:1 + 2 * twos:2], tallies[2:2 + 2 * twos:2]
    slack = jnp.minimum(donor - 1, limit - taker)
    moved = jax.random.randint(jax.random.fold_in(own_key, 1), (twos,), 0, 1 << 20) % (slack + 1)
    tallies = tallies.at[1:1 + 2 * twos:2].set(donor - moved).at[2:2 + 2 * twos:2].set(taker + moved)
    return tallies[jax.random.permutation(jax.random.fold_in(own_key, 2), amount)]


def bell_draw(own_key, dims, spread, limit, cuts=(), kind=jnp.bfloat16):
    array = spread * jax.random.normal(own_key, dims, jnp.float32)
    if cuts:
        array = array * levels(own_key, dims, cuts, -0.22, 0.18)
    return jnp.clip(array, -limit, limit).astype(kind)


def setup_inputs(seed: int = 0) -> dict:
    splits = jax.random.split(jax.random.key(seed), 25)
    return {
        "tokens": bell_draw(splits[0], (SEQS, LEN, D), 1.0, 6.0, ((0, 4), (1, 2)), jnp.float32),
        "cotangent": bell_draw(splits[1], (SEQS, LEN, D), 1.0, 6.0, ((0, 4), (1, 2)), jnp.float32),
        "doc_lengths": jax.vmap(lambda own: uneven(own, NDOC, LEN, LEN // 4, 2))(jax.random.split(splits[2], SEQS)).reshape((SEQS, NDOC)).astype(jnp.int32),
        "norm1_gain": jnp.clip(1.0 + 0.1 * jax.random.normal(splits[3], (D,), jnp.float32), 0.5, 1.5),
        "in_weight": bell_draw(splits[4], (3, D, D), D ** -0.5, 0.1875, ((1, 8), (2, 4)), jnp.float32),
        "conv_weight": bell_draw(splits[5], (TAPS, D), TAPS ** -0.5, 3.5, ((1, 4),), jnp.float32),
        "out_weight": bell_draw(splits[6], (D, D), D ** -0.5, 0.1875, ((0, 4), (1, 8)), jnp.float32),
        "norm2_gain": jnp.clip(1.0 + 0.1 * jax.random.normal(splits[7], (D,), jnp.float32), 0.5, 1.5),
        "gate_up_weight": bell_draw(splits[8], (2, D, FF), D ** -0.5, 0.1875, ((1, 8), (2, 4)), jnp.float32),
        "down_weight": bell_draw(splits[9], (FF, D), FF ** -0.5, 0.09375, ((0, 4), (1, 8)), jnp.float32),
        "first_norm1": bell_draw(splits[10], (D,), 1.0, 6.0, ((0, 8),), jnp.float32),
        "first_in": bell_draw(splits[11], (3, D, D), 1.0, 6.0, ((1, 8), (2, 4)), jnp.float32),
        "first_conv": bell_draw(splits[12], (TAPS, D), 1.0, 6.0, ((1, 4),), jnp.float32),
        "first_out": bell_draw(splits[13], (D, D), 1.0, 6.0, ((0, 4), (1, 8)), jnp.float32),
        "first_norm2": bell_draw(splits[14], (D,), 1.0, 6.0, ((0, 8),), jnp.float32),
        "first_gate_up": bell_draw(splits[15], (2, D, FF), 1.0, 6.0, ((1, 8), (2, 4)), jnp.float32),
        "first_down": bell_draw(splits[16], (FF, D), 1.0, 6.0, ((0, 4), (1, 8)), jnp.float32),
        "second_norm1": jnp.clip(jnp.exp(math.log(100.0) - 4.6051702 * jax.random.uniform(splits[17], (D,), jnp.float32) ** levels(splits[17], (D,), ((0, 8),), -0.2, 0.2)), 1.0, 100.0),
        "second_in": jnp.clip(jnp.exp(math.log(100.0) - 4.6051702 * jax.random.uniform(splits[18], (3, D, D), jnp.float32) ** levels(splits[18], (3, D, D), ((1, 8), (2, 4)), -0.2, 0.2)), 1.0, 100.0),
        "second_conv": jnp.clip(jnp.exp(math.log(100.0) - 4.6051702 * jax.random.uniform(splits[19], (TAPS, D), jnp.float32) ** levels(splits[19], (TAPS, D), ((1, 4),), -0.2, 0.2)), 1.0, 100.0),
        "second_out": jnp.clip(jnp.exp(math.log(100.0) - 4.6051702 * jax.random.uniform(splits[20], (D, D), jnp.float32) ** levels(splits[20], (D, D), ((0, 4), (1, 8)), -0.2, 0.2)), 1.0, 100.0),
        "second_norm2": jnp.clip(jnp.exp(math.log(100.0) - 4.6051702 * jax.random.uniform(splits[21], (D,), jnp.float32) ** levels(splits[21], (D,), ((0, 8),), -0.2, 0.2)), 1.0, 100.0),
        "second_gate_up": jnp.clip(jnp.exp(math.log(100.0) - 4.6051702 * jax.random.uniform(splits[22], (2, D, FF), jnp.float32) ** levels(splits[22], (2, D, FF), ((1, 8), (2, 4)), -0.2, 0.2)), 1.0, 100.0),
        "second_down": jnp.clip(jnp.exp(math.log(100.0) - 4.6051702 * jax.random.uniform(splits[23], (FF, D), jnp.float32) ** levels(splits[23], (FF, D), ((0, 4), (1, 8)), -0.2, 0.2)), 1.0, 100.0),
    }


EPS_NORM = 1e-05
BETA_ONE = 0.9
BETA_TWO = 0.95
LEARN_RATE = 0.01
DECAY_RATE = 0.1
ADAM_EPS = 1e-08

def doc_masks(lengths_row, begin, count):
    positions = begin + jnp.arange(count, dtype=jnp.int32)
    lengths_row = lengths_row.astype(jnp.int32)
    starts = jnp.cumsum(lengths_row).astype(jnp.int32) - lengths_row
    inside = starts[None, :] <= positions[:, None]
    doc_start = lax.optimization_barrier(jnp.max(jnp.where(inside, starts[None, :], jnp.int32(0)), axis=1))
    mask_one = (positions - 1 >= doc_start).astype(jnp.float32)[:, None]
    mask_two = (positions - 2 >= doc_start).astype(jnp.float32)[:, None]
    return (mask_one, mask_two)

def shifted(values, lag):
    zeros = jnp.zeros((lag, values.shape[1]), jnp.float32)
    return jnp.concatenate([zeros, values[:-lag]], axis=0)

def leading(values, lag):
    zeros = jnp.zeros((lag, values.shape[1]), jnp.float32)
    return jnp.concatenate([values[lag:], zeros], axis=0)

def rms_scale(inputs):
    return lax.rsqrt(lax.optimization_barrier(jnp.mean(inputs * inputs, axis=-1, keepdims=True)) + EPS_NORM)

def norm_back(grad_normed, unit_rows, gain_full, scale_rows):
    scaled = grad_normed * gain_full
    return scale_rows * (scaled - unit_rows * lax.optimization_barrier(jnp.mean(scaled * unit_rows, axis=-1, keepdims=True)))

def block_sums(lefts, rights, parts):
    width = lefts[0].shape[1] // parts
    total = jnp.zeros((lefts[0].shape[0], rights[0].shape[0]), jnp.float32)
    for block in range(parts):
        term = jnp.zeros_like(total)
        for left, right in zip(lefts, rights):
            term = term + jnp.dot(left[:, block * width:(block + 1) * width], right[:, block * width:(block + 1) * width].T, preferred_element_type=jnp.float32)
        total = total + lax.optimization_barrier(term.astype(jnp.bfloat16)).astype(jnp.float32)
    return total

def per_sequence(rows, upstream_f, lengths_row, gain_one, gain_two, w_in, conv_weight, w_out, w_gate_up, w_down):
    length = rows.shape[0]
    mask_one, mask_two = doc_masks(lengths_row, 0, length)
    scale_one = rms_scale(rows)
    unit_one = rows * scale_one
    normed_one = (unit_one * gain_one).astype(jnp.bfloat16)
    gate_b = jnp.dot(normed_one, w_in[0], preferred_element_type=jnp.float32)
    gate_c = jnp.dot(normed_one, w_in[1], preferred_element_type=jnp.float32)
    values_x = jnp.dot(normed_one, w_in[2], preferred_element_type=jnp.float32)
    mixed_in = gate_b * values_x
    lag_one = shifted(mixed_in, 1) * mask_one
    lag_two = shifted(mixed_in, 2) * mask_two
    conv_out = conv_weight[0] * lag_two + conv_weight[1] * lag_one + conv_weight[2] * mixed_in
    gated_y = (gate_c * conv_out).astype(jnp.bfloat16)
    mixer_out = jnp.dot(gated_y, w_out, preferred_element_type=jnp.float32)
    hidden_rows = rows + mixer_out
    scale_two = rms_scale(hidden_rows)
    unit_two = hidden_rows * scale_two
    normed_two = (unit_two * gain_two).astype(jnp.bfloat16)
    gate_pre = jnp.dot(normed_two, w_gate_up[0], preferred_element_type=jnp.float32)
    up_pre = jnp.dot(normed_two, w_gate_up[1], preferred_element_type=jnp.float32)
    sig = jax.nn.sigmoid(gate_pre)
    activated = (gate_pre * sig * up_pre).astype(jnp.bfloat16)
    result = hidden_rows + jnp.dot(activated, w_down, preferred_element_type=jnp.float32)
    upstream = upstream_f.astype(jnp.bfloat16)
    grad_act = jnp.dot(upstream, w_down.T, preferred_element_type=jnp.float32)
    grad_down = jnp.dot(activated.T, upstream, preferred_element_type=jnp.float32)
    grad_gate = (grad_act * up_pre * sig * (1.0 + gate_pre * (1.0 - sig))).astype(jnp.bfloat16)
    grad_up = (grad_act * gate_pre * sig).astype(jnp.bfloat16)
    grad_gate_up = jnp.stack([jnp.dot(normed_two.T, grad_gate, preferred_element_type=jnp.float32), jnp.dot(normed_two.T, grad_up, preferred_element_type=jnp.float32)])
    grad_normed_two = block_sums((grad_gate, grad_up), (w_gate_up[0], w_gate_up[1]), N_TP)
    grad_norm2 = lax.optimization_barrier(jnp.sum(grad_normed_two * unit_two, axis=0))
    grad_hidden = upstream_f + norm_back(grad_normed_two, unit_two, gain_two, scale_two)
    grad_hidden_b = grad_hidden.astype(jnp.bfloat16)
    grad_y = jnp.dot(grad_hidden_b, w_out.T, preferred_element_type=jnp.float32)
    grad_out = jnp.dot(gated_y.T, grad_hidden_b, preferred_element_type=jnp.float32)
    grad_c = grad_y * conv_out
    grad_conv_in = grad_y * gate_c
    grad_mixed = conv_weight[2] * grad_conv_in + conv_weight[1] * leading(grad_conv_in * mask_one, 1) + conv_weight[0] * leading(grad_conv_in * mask_two, 2)
    grad_conv = jnp.stack([lax.optimization_barrier(jnp.sum(grad_conv_in * lag_two, axis=0)), lax.optimization_barrier(jnp.sum(grad_conv_in * lag_one, axis=0)), lax.optimization_barrier(jnp.sum(grad_conv_in * mixed_in, axis=0))])
    grad_gb = (grad_mixed * values_x).astype(jnp.bfloat16)
    grad_gc = grad_c.astype(jnp.bfloat16)
    grad_gx = (grad_mixed * gate_b).astype(jnp.bfloat16)
    grad_in = jnp.stack([jnp.dot(normed_one.T, grad_gb, preferred_element_type=jnp.float32), jnp.dot(normed_one.T, grad_gc, preferred_element_type=jnp.float32), jnp.dot(normed_one.T, grad_gx, preferred_element_type=jnp.float32)])
    grad_normed_one = block_sums((grad_gb, grad_gc, grad_gx), (w_in[0], w_in[1], w_in[2]), N_TP)
    grad_norm1 = lax.optimization_barrier(jnp.sum(grad_normed_one * unit_one, axis=0))
    grad_tokens = grad_hidden + norm_back(grad_normed_one, unit_one, gain_one, scale_one)
    return (result, grad_tokens, (grad_norm1, grad_in, grad_conv, grad_out, grad_norm2, grad_gate_up, grad_down))

def adamw(param, grads, first, second, bias_one, bias_two):
    new_first = BETA_ONE * first + (1.0 - BETA_ONE) * grads
    new_second = BETA_TWO * second + (1.0 - BETA_TWO) * grads * grads
    update = new_first / bias_one / (jnp.sqrt(new_second / bias_two) + ADAM_EPS) + DECAY_RATE * param
    return (param - LEARN_RATE * update, new_first, new_second)

def reference(tokens, cotangent, doc_lengths, norm1_gain, in_weight, conv_weight, out_weight, norm2_gain, gate_up_weight, down_weight, first_norm1, first_in, first_conv, first_out, first_norm2, first_gate_up, first_down, second_norm1, second_in, second_conv, second_out, second_norm2, second_gate_up, second_down):
    gain_one = lax.optimization_barrier(norm1_gain.astype(jnp.bfloat16)).astype(jnp.float32)
    gain_two = lax.optimization_barrier(norm2_gain.astype(jnp.bfloat16)).astype(jnp.float32)
    w_in = in_weight.astype(jnp.bfloat16)
    w_out = out_weight.astype(jnp.bfloat16)
    w_gate_up = gate_up_weight.astype(jnp.bfloat16)
    w_down = down_weight.astype(jnp.bfloat16)

    def one_sequence(carry, inputs):
        rows, upstream_f, lengths_row = inputs
        result, grad_tokens, grads = per_sequence(rows, upstream_f, lengths_row, gain_one, gain_two, w_in, conv_weight, w_out, w_gate_up, w_down)
        return (jax.tree.map(jnp.add, carry, grads), (result, grad_tokens))
    zeros_init = (jnp.zeros(norm1_gain.shape, jnp.float32), jnp.zeros(in_weight.shape, jnp.float32), jnp.zeros(conv_weight.shape, jnp.float32), jnp.zeros(out_weight.shape, jnp.float32), jnp.zeros(norm2_gain.shape, jnp.float32), jnp.zeros(gate_up_weight.shape, jnp.float32), jnp.zeros(down_weight.shape, jnp.float32))
    totals, outputs = lax.scan(one_sequence, zeros_init, (tokens, cotangent, doc_lengths))
    result, grad_tokens = outputs
    grad_norm1, grad_in, grad_conv, grad_out, grad_norm2, grad_gate_up, grad_down = totals
    count = jnp.float32(STEP)
    bias_one = 1.0 - jnp.power(jnp.float32(BETA_ONE), count)
    bias_two = 1.0 - jnp.power(jnp.float32(BETA_TWO), count)
    new_norm1, new_first_norm1, new_second_norm1 = adamw(norm1_gain, grad_norm1, first_norm1, second_norm1, bias_one, bias_two)
    new_in, new_first_in, new_second_in = adamw(in_weight, grad_in, first_in, second_in, bias_one, bias_two)
    new_conv, new_first_conv, new_second_conv = adamw(conv_weight, grad_conv, first_conv, second_conv, bias_one, bias_two)
    new_out, new_first_out, new_second_out = adamw(out_weight, grad_out, first_out, second_out, bias_one, bias_two)
    new_norm2, new_first_norm2, new_second_norm2 = adamw(norm2_gain, grad_norm2, first_norm2, second_norm2, bias_one, bias_two)
    new_gate_up, new_first_gate_up, new_second_gate_up = adamw(gate_up_weight, grad_gate_up, first_gate_up, second_gate_up, bias_one, bias_two)
    new_down, new_first_down, new_second_down = adamw(down_weight, grad_down, first_down, second_down, bias_one, bias_two)
    return (result, grad_tokens, grad_norm1, grad_in, grad_conv, grad_out, grad_norm2, grad_gate_up, grad_down, new_norm1, new_in, new_conv, new_out, new_norm2, new_gate_up, new_down, new_first_norm1, new_first_in, new_first_conv, new_first_out, new_first_norm2, new_first_gate_up, new_first_down, new_second_norm1, new_second_in, new_second_conv, new_second_out, new_second_norm2, new_second_gate_up, new_second_down)
```

```python
import jax
import jax.numpy as jnp
from jax import lax
from jax.sharding import Mesh, PartitionSpec as P

STEP = 5


EPS_NORM = 1e-05
BETA_ONE = 0.9
BETA_TWO = 0.95
LEARN_RATE = 0.01
DECAY_RATE = 0.1
ADAM_EPS = 1e-08

DATA = ("dp", "ctx")
MODEL = ("lo", "hi")


bf16 = jnp.bfloat16
f32 = jnp.float32


def doc_masks(lengths_row, count):
    positions = jnp.arange(count, dtype=jnp.int32)
    starts = jnp.cumsum(lengths_row) - lengths_row
    inside = starts[None, :] <= positions[:, None]
    doc_start = jnp.max(jnp.where(inside, starts[None, :], jnp.int32(0)), axis=1)
    mask_one = (positions - 1 >= doc_start).astype(f32)[:, None]
    mask_two = (positions - 2 >= doc_start).astype(f32)[:, None]
    return (mask_one, mask_two)


def rms_scale(inputs):
    return lax.rsqrt(jnp.mean(inputs * inputs, axis=-1, keepdims=True) + EPS_NORM)


def norm_back(grad_normed, unit_rows, gain_full, scale_rows):
    scaled = grad_normed * gain_full
    return scale_rows * (scaled - unit_rows * jnp.mean(scaled * unit_rows, axis=-1, keepdims=True))


def adamw(param, grads, first, second, bias_one, bias_two):
    new_first = BETA_ONE * first + (1.0 - BETA_ONE) * grads
    new_second = BETA_TWO * second + (1.0 - BETA_TWO) * grads * grads
    update = (
        new_first / bias_one / (jnp.sqrt(new_second / bias_two) + ADAM_EPS) + DECAY_RATE * param
    )
    return (param - LEARN_RATE * update, new_first, new_second)


def exchange(blocks, axes):
    return lax.all_to_all(blocks, axes, 0, 0, tiled=True)


def swap(block, axis):
    return lax.ppermute(block, axis, [(0, 1), (1, 0)])


def gather(block, axis):
    if lax.axis_size(axis) == 2:
        other = swap(block, axis)
        first = lax.axis_index(axis) == 0
        return jnp.stack([jnp.where(first, block, other), jnp.where(first, other, block)])
    return lax.all_gather(block, axis)


def sum_scatter(blocks, axis):
    if lax.axis_size(axis) == 2:
        mine = lax.axis_index(axis)
        kept = lax.dynamic_index_in_dim(blocks, mine, 0, keepdims=False)
        given = lax.dynamic_index_in_dim(blocks, 1 - mine, 0, keepdims=False)
        return kept.astype(f32) + swap(given, axis).astype(f32)
    return jnp.sum(exchange(blocks, axis).astype(f32), axis=0)


def gather_features(block):
    return lax.all_gather(block, MODEL, axis=block.ndim - 1, tiled=True)


def per_device(
    tokens,
    cotangent,
    doc_lengths,
    norm1_gain,
    in_weight,
    conv_weight,
    out_weight,
    norm2_gain,
    gate_up_weight,
    down_weight,
    first_norm1,
    first_in,
    first_conv,
    first_out,
    first_norm2,
    first_gate_up,
    first_down,
    second_norm1,
    second_in,
    second_conv,
    second_out,
    second_norm2,
    second_gate_up,
    second_down,
):
    n_dp = lax.axis_size("dp")
    n_ctx = lax.axis_size("ctx")
    n_hi = lax.axis_size("hi")
    n_lo = lax.axis_size("lo")
    n_tp = n_hi * n_lo
    n_data = n_dp * n_ctx
    at_ctx = lax.axis_index("ctx")
    at_lo = lax.axis_index("lo")

    rows = tokens.reshape(-1, tokens.shape[-1])
    upstream_f = cotangent.reshape(rows.shape)
    count, width = rows.shape
    length = count * n_ctx
    d_own = in_weight.shape[1]
    c_tp = in_weight.shape[2]
    c_own = c_tp // n_ctx
    f_tp = down_weight.shape[0]
    f_own = f_tp // n_dp
    half = width // n_lo
    quarter = width // n_tp

    mixer_own = jnp.concatenate([in_weight, out_weight.T[None]]).astype(bf16)
    mixer_own = mixer_own.reshape(4, d_own, n_ctx, c_own).transpose(2, 0, 1, 3)
    mixer_own = mixer_own.reshape(n_ctx, 4 * d_own, c_own)
    gains = jnp.concatenate([norm1_gain, norm2_gain]).astype(bf16)
    pad = -gains.shape[0] % c_own
    gains = jnp.pad(gains, (0, pad)).reshape(-1, c_own)
    gains_all = exchange(jnp.broadcast_to(gains[None], (n_data, *gains.shape)), DATA)
    gains_all = gains_all.reshape(n_data, -1)[:, : 2 * d_own].astype(f32)
    gain_one = gains_all[:, :d_own].reshape(width)
    gain_two = gains_all[:, d_own:].reshape(width)

    scale_one = rms_scale(rows)
    unit_one = rows * scale_one
    normed_one = (unit_one * gain_one).astype(bf16)
    normed_seq = gather(normed_one, "ctx").reshape(length, width)

    ffn_own = jnp.concatenate(
        [gate_up_weight.astype(bf16).transpose(0, 2, 1), down_weight.astype(bf16)[None]]
    )
    ffn_own = ffn_own.reshape(3, n_dp, f_own, d_own).transpose(1, 0, 2, 3)
    ffn_got = exchange(ffn_own, "dp")
    ffn_all = gather(ffn_got, "ctx")
    w_ffn = ffn_all.transpose(2, 3, 1, 0, 4).reshape(3, f_own, width)
    w_gate_up = w_ffn[:2]
    w_down = w_ffn[2]

    mixer_all = exchange(
        jnp.broadcast_to(mixer_own[None], (n_dp, *mixer_own.shape)).reshape(
            n_data, *mixer_own.shape[1:]
        ),
        DATA,
    )
    w_mixer = mixer_all.reshape(n_data, 4, d_own, c_own).transpose(1, 0, 2, 3)
    w_mixer = w_mixer.reshape(4, width, c_own)
    w_in = w_mixer[:3]
    w_out = w_mixer[3]

    def gather_rows(block):
        part = lax.dynamic_slice_in_dim(block, at_lo * half, half, 1)
        parts = exchange(jnp.broadcast_to(part[None], (n_dp, *part.shape)), "dp")
        whole = gather(parts.reshape(n_dp * count, half), "lo")
        return whole.transpose(1, 0, 2).reshape(n_dp * count, width)

    upstream = gather_rows(upstream_f.astype(bf16))

    mask_one, mask_two = doc_masks(doc_lengths[0], length + 2)
    taps = lax.dynamic_slice_in_dim(conv_weight, at_ctx * c_own, c_own, 1)
    projected = jnp.einsum("td,kdc->ktc", normed_seq, w_in, preferred_element_type=f32)
    gate_b = projected[0]
    gate_c = projected[1]
    values_x = projected[2]
    mixed_in = gate_b * values_x
    extended = jnp.pad(mixed_in, ((2, 0), (0, 0)))
    lag_one = extended[1 : length + 1] * mask_one[:length]
    lag_two = extended[:length] * mask_two[:length]
    conv_out = taps[0] * lag_two + taps[1] * lag_one + taps[2] * mixed_in
    gated_y = (gate_c * conv_out).astype(bf16)

    def mixer_sum(part):
        blocks = part.astype(bf16).reshape(n_ctx, count, n_tp, quarter).transpose(0, 2, 1, 3)
        blocks = exchange(blocks.reshape(n_ctx * n_tp, count, quarter), ("ctx", *MODEL))
        return jnp.sum(blocks.astype(f32), axis=0)

    mixer_part = lax.dot_general(
        gated_y, w_out, (((1,), (1,)), ((), ())), preferred_element_type=f32
    )
    mixer_out = gather_features(mixer_sum(mixer_part).astype(bf16)).astype(f32)
    hidden_rows = rows + mixer_out
    scale_two = rms_scale(hidden_rows)
    unit_two = hidden_rows * scale_two
    normed_two = gather_rows((unit_two * gain_two).astype(bf16))

    gate_up = jnp.einsum("td,kfd->ktf", normed_two, w_gate_up, preferred_element_type=f32)
    gate_pre = gate_up[0]
    up_pre = gate_up[1]
    sig = jax.nn.sigmoid(gate_pre)
    activated = (gate_pre * sig * up_pre).astype(bf16)
    grad_act = lax.dot_general(
        upstream, w_down, (((1,), (1,)), ((), ())), preferred_element_type=f32
    )
    grad_gate = (grad_act * up_pre * sig * (1.0 + gate_pre * (1.0 - sig))).astype(bf16)
    grad_up = (grad_act * gate_pre * sig).astype(bf16)
    both_grads = jnp.stack([grad_gate, grad_up])
    ffn_part = jnp.dot(activated, w_down, preferred_element_type=f32)
    normed_two_part = jnp.einsum("ktf,kfd->td", both_grads, w_gate_up, preferred_element_type=f32)

    parts = jnp.stack([ffn_part.astype(bf16), normed_two_part.astype(bf16)])
    parts = parts.reshape(2, n_dp * count, n_lo, half).transpose(2, 0, 1, 3)
    parts = sum_scatter(parts, "lo").astype(bf16)
    parts = parts.reshape(2, n_dp, count, n_hi, quarter).transpose(1, 3, 0, 2, 4)
    parts = exchange(parts.reshape(n_dp * n_hi, 2, count, quarter), ("dp", "hi"))
    parts = jnp.sum(parts.astype(f32), axis=0).astype(bf16)
    parts = gather_features(parts).astype(f32)
    result = hidden_rows + parts[0]
    grad_normed_two = parts[1]

    grad_gate_up = jnp.einsum("ktf,td->kfd", both_grads, normed_two, preferred_element_type=f32)
    grad_down = lax.dot_general(
        activated, upstream, (((0,), (0,)), ((), ())), preferred_element_type=f32
    )
    grad_ffn = jnp.concatenate([grad_gate_up.astype(bf16), grad_down.astype(bf16)[None]])
    grad_ffn = grad_ffn.reshape(3, f_own, n_dp, n_ctx, d_own).transpose(3, 2, 0, 1, 4)
    grad_ffn = sum_scatter(grad_ffn, "ctx").astype(bf16)
    grad_ffn = exchange(grad_ffn, "dp").transpose(1, 0, 2, 3).reshape(3, f_tp, d_own).astype(f32)
    owned_gate_up = grad_ffn[:2].transpose(0, 2, 1)
    owned_down = grad_ffn[2]

    grad_norm2 = jnp.sum(grad_normed_two * unit_two, axis=0)
    grad_hidden = upstream_f + norm_back(grad_normed_two, unit_two, gain_two, scale_two)
    grad_seq = gather(grad_hidden.astype(bf16), "ctx").reshape(length, width)

    grad_y = jnp.dot(grad_seq, w_out, preferred_element_type=f32)
    grad_out = lax.dot_general(
        grad_seq, gated_y, (((0,), (0,)), ((), ())), preferred_element_type=f32
    )
    grad_c = grad_y * conv_out
    grad_conv_in = grad_y * gate_c
    grad_ext = jnp.pad(grad_conv_in, ((0, 2), (0, 0)))
    lead_one = (grad_ext * mask_one)[1 : length + 1]
    lead_two = (grad_ext * mask_two)[2:]
    grad_mixed = taps[2] * grad_conv_in + taps[1] * lead_one + taps[0] * lead_two
    grad_taps = jnp.stack(
        [
            jnp.sum(grad_conv_in * lag_two, axis=0),
            jnp.sum(grad_conv_in * lag_one, axis=0),
            jnp.sum(grad_conv_in * mixed_in, axis=0),
        ]
    )
    grad_gates = jnp.stack(
        [
            (grad_mixed * values_x).astype(bf16),
            grad_c.astype(bf16),
            (grad_mixed * gate_b).astype(bf16),
        ]
    )
    normed_one_part = jnp.einsum("ktc,kdc->td", grad_gates, w_in, preferred_element_type=f32)
    grad_normed_one = gather_features(mixer_sum(normed_one_part).astype(bf16)).astype(f32)
    grad_norm1 = jnp.sum(grad_normed_one * unit_one, axis=0)
    grad_tokens = grad_hidden + norm_back(grad_normed_one, unit_one, gain_one, scale_one)

    grad_in = jnp.einsum("td,ktc->kdc", normed_seq, grad_gates, preferred_element_type=f32)
    grad_mixer = jnp.concatenate([grad_in.astype(bf16), grad_out.astype(bf16)[None]])
    grad_mixer = grad_mixer.reshape(4, n_data, d_own, c_own).transpose(1, 0, 2, 3)
    grad_mixer = grad_mixer.reshape(n_data, 4 * d_own, c_own)
    small = jnp.concatenate(
        [
            grad_norm1.reshape(n_data, d_own),
            grad_norm2.reshape(n_data, d_own),
            jnp.broadcast_to(grad_taps.reshape(1, -1), (n_data, grad_taps.size)),
        ],
        axis=1,
    ).astype(bf16)
    n_small = small.shape[1]
    small = jnp.pad(small, ((0, 0), (0, -n_small % c_own))).reshape(n_data, -1, c_own)
    mixed = exchange(jnp.concatenate([grad_mixer, small], axis=1), DATA).astype(f32)
    mixed = mixed.reshape(n_dp, n_ctx, -1, c_own)
    owned_mixer = jnp.sum(mixed[:, :, : 4 * d_own], axis=0).reshape(n_ctx, 4, d_own, c_own)
    owned_mixer = owned_mixer.transpose(1, 2, 0, 3).reshape(4, d_own, c_tp)
    owned_in = owned_mixer[:3]
    owned_out = owned_mixer[3].T
    small = jnp.sum(mixed[:, :, 4 * d_own :], axis=0).reshape(n_ctx, -1)
    owned_norm1 = jnp.sum(small[:, :d_own], axis=0)
    owned_norm2 = jnp.sum(small[:, d_own : 2 * d_own], axis=0)
    grad_conv = small[:, 2 * d_own : n_small].reshape(n_ctx, 3, c_own)
    grad_conv = grad_conv.transpose(1, 0, 2).reshape(3, c_tp)

    steps = jnp.float32(STEP)
    bias_one = 1.0 - jnp.power(jnp.float32(BETA_ONE), steps)
    bias_two = 1.0 - jnp.power(jnp.float32(BETA_TWO), steps)
    new_norm1, new_first_norm1, new_second_norm1 = adamw(
        norm1_gain, owned_norm1, first_norm1, second_norm1, bias_one, bias_two
    )
    new_in, new_first_in, new_second_in = adamw(
        in_weight, owned_in, first_in, second_in, bias_one, bias_two
    )
    new_conv, new_first_conv, new_second_conv = adamw(
        conv_weight, grad_conv, first_conv, second_conv, bias_one, bias_two
    )
    new_out, new_first_out, new_second_out = adamw(
        out_weight, owned_out, first_out, second_out, bias_one, bias_two
    )
    new_norm2, new_first_norm2, new_second_norm2 = adamw(
        norm2_gain, owned_norm2, first_norm2, second_norm2, bias_one, bias_two
    )
    new_gate_up, new_first_gate_up, new_second_gate_up = adamw(
        gate_up_weight, owned_gate_up, first_gate_up, second_gate_up, bias_one, bias_two
    )
    new_down, new_first_down, new_second_down = adamw(
        down_weight, owned_down, first_down, second_down, bias_one, bias_two
    )
    return (
        result.reshape(tokens.shape),
        grad_tokens.reshape(tokens.shape),
        owned_norm1,
        owned_in,
        grad_conv,
        owned_out,
        owned_norm2,
        owned_gate_up,
        owned_down,
        new_norm1,
        new_in,
        new_conv,
        new_out,
        new_norm2,
        new_gate_up,
        new_down,
        new_first_norm1,
        new_first_in,
        new_first_conv,
        new_first_out,
        new_first_norm2,
        new_first_gate_up,
        new_first_down,
        new_second_norm1,
        new_second_in,
        new_second_conv,
        new_second_out,
        new_second_norm2,
        new_second_gate_up,
        new_second_down,
    )


def solution(mesh):
    n_dp, n_ctx, n_tp = (mesh.shape[name] for name in ("dp", "ctx", "tp"))
    n_lo = 2 if n_tp % 2 == 0 else 1
    devices = mesh.devices.reshape(n_dp, n_ctx, n_tp // n_lo, n_lo)
    paired = Mesh(devices, ("dp", "ctx", "hi", "lo"))
    tp = ("hi", "lo")

    row = P("dp", "ctx", None)
    params = (
        P(DATA),
        P(None, DATA, tp),
        P(None, tp),
        P(tp, DATA),
        P(DATA),
        P(None, DATA, tp),
        P(tp, DATA),
    )
    return jax.shard_map(
        per_device,
        mesh=paired,
        in_specs=(row, row, P("dp", None), *params, *params, *params),
        out_specs=(row, row, *params, *params, *params, *params),
        check_vma=False,
    )
```

```python
import jax
import jax.numpy as jnp
from jax import lax
from jax.experimental import pallas as pl
from jax.experimental.layout import Layout, with_layout_constraint
from jax.experimental.pallas import tpu as pltpu
from jax.sharding import Mesh, PartitionSpec as P

STEP = 5


EPS_NORM = 1e-05
BETA_ONE = 0.9
BETA_TWO = 0.95
LEARN_RATE = 0.01
DECAY_RATE = 0.1
ADAM_EPS = 1e-08

DATA = ("dp", "ctx")
MODEL = ("lo", "hi")


bf16 = jnp.bfloat16
f32 = jnp.float32


def doc_masks(lengths_row, count):
    positions = jnp.arange(count, dtype=jnp.int32)
    starts = jnp.cumsum(lengths_row) - lengths_row
    inside = starts[None, :] <= positions[:, None]
    doc_start = jnp.max(jnp.where(inside, starts[None, :], jnp.int32(0)), axis=1)
    mask_one = (positions - 1 >= doc_start).astype(f32)[:, None]
    mask_two = (positions - 2 >= doc_start).astype(f32)[:, None]
    return (mask_one, mask_two)


def rms_scale(inputs):
    return lax.rsqrt(jnp.mean(inputs * inputs, axis=-1, keepdims=True) + EPS_NORM)


def norm_back(grad_normed, unit_rows, gain_full, scale_rows):
    scaled = grad_normed * gain_full
    return scale_rows * (scaled - unit_rows * jnp.mean(scaled * unit_rows, axis=-1, keepdims=True))


def adamw(param, grads, first, second, bias_one, bias_two):
    new_first = BETA_ONE * first + (1.0 - BETA_ONE) * grads
    new_second = BETA_TWO * second + (1.0 - BETA_TWO) * grads * grads
    update = (
        new_first / bias_one / (jnp.sqrt(new_second / bias_two) + ADAM_EPS) + DECAY_RATE * param
    )
    return (param - LEARN_RATE * update, new_first, new_second)


def exchange(blocks, axes):
    return lax.all_to_all(blocks, axes, 0, 0, tiled=True)


def swap(block, axis):
    return lax.ppermute(block, axis, [(0, 1), (1, 0)])


def gather(block, axis):
    if lax.axis_size(axis) == 2:
        other = swap(block, axis)
        first = lax.axis_index(axis) == 0
        return jnp.stack([jnp.where(first, block, other), jnp.where(first, other, block)])
    return lax.all_gather(block, axis)


def sum_scatter(blocks, axis):
    if lax.axis_size(axis) == 2:
        mine = lax.axis_index(axis)
        kept = lax.dynamic_index_in_dim(blocks, mine, 0, keepdims=False)
        given = lax.dynamic_index_in_dim(blocks, 1 - mine, 0, keepdims=False)
        return kept.astype(f32) + swap(given, axis).astype(f32)
    return jnp.sum(exchange(blocks, axis).astype(f32), axis=0)


def gather_last(block, axis):
    if lax.axis_size(axis) == 2:
        other = swap(block, axis)
        first = lax.axis_index(axis) == 0
        return jnp.concatenate(
            [jnp.where(first, block, other), jnp.where(first, other, block)], axis=-1
        )
    return lax.all_gather(block, axis, axis=block.ndim - 1, tiled=True)


def gather_features(block):
    return gather_last(gather_last(block, "hi"), "lo")


def row_major(block):
    return with_layout_constraint(block, Layout(major_to_minor=tuple(range(block.ndim))))


def dot_nt(left, right):
    return lax.dot_general(left, right, (((1,), (1,)), ((), ())), preferred_element_type=f32)


def dot_tn(left, right):
    return lax.dot_general(left, right, (((0,), (0,)), ((), ())), preferred_element_type=f32)


def ffn_body(
    at, normed_own, normed_other, up_own, up_other, w_own, w_other,
    kept_rows, given_rows, kept_grads, given_grads,
    normed, upstream, weights, act, grad_gate, grad_up,
):
    n_dp, f_three, lane = w_own.shape
    f_own = f_three // 3
    rows, half = normed_own.shape
    count = rows // n_dp
    n_hi = kept_rows.shape[1]
    quarter = half // n_hi
    ctx_first = at[0] == 0
    lo_first = at[1] == 0

    def place(even, odd):
        for z in range(n_dp):
            weights[:, 2 * z * lane : (2 * z + 1) * lane] = even[z]
            weights[:, (2 * z + 1) * lane : (2 * z + 2) * lane] = odd[z]

    @pl.when(ctx_first)
    def _():
        place(w_own, w_other)

    @pl.when(jnp.logical_not(ctx_first))
    def _():
        place(w_other, w_own)

    @pl.when(lo_first)
    def _():
        normed[:, :half] = normed_own[...]
        normed[:, half:] = normed_other[...]
        upstream[:, :half] = up_own[...]
        upstream[:, half:] = up_other[...]

    @pl.when(jnp.logical_not(lo_first))
    def _():
        normed[:, :half] = normed_other[...]
        normed[:, half:] = normed_own[...]
        upstream[:, :half] = up_other[...]
        upstream[:, half:] = up_own[...]

    tiles = 2
    tile = rows // tiles

    def step(i, carry):
        part = pl.ds(pl.multiple_of(i * tile, tile), tile)
        n_rows = normed[part, :]
        gate_pre = dot_nt(n_rows, weights[:f_own, :])
        up_pre = dot_nt(n_rows, weights[f_own : 2 * f_own, :])
        grad_act = dot_nt(upstream[part, :], weights[2 * f_own :, :])
        sig = 1.0 / (1.0 + jnp.exp(-gate_pre))
        gated = gate_pre * sig
        act[part, :] = (gated * up_pre).astype(bf16)
        grad_gate[part, :] = (grad_act * up_pre * sig * (1.0 + gate_pre * (1.0 - sig))).astype(bf16)
        grad_up[part, :] = (grad_act * gated).astype(bf16)

        def send(which, values):
            kept = jnp.where(lo_first, values[:, :half], values[:, half:]).astype(bf16)
            given = jnp.where(lo_first, values[:, half:], values[:, :half]).astype(bf16)
            for j in range(n_dp // tiles):
                z = i * (n_dp // tiles) + j
                for h in range(n_hi):
                    cut = (slice(j * count, (j + 1) * count), slice(h * quarter, (h + 1) * quarter))
                    kept_rows[z, h, which] = kept[cut]
                    given_rows[z, h, which] = given[cut]

        send(0, jnp.dot(act[part, :], weights[2 * f_own :, :], preferred_element_type=f32))
        send(
            1,
            jnp.dot(grad_gate[part, :], weights[:f_own, :], preferred_element_type=f32)
            + jnp.dot(grad_up[part, :], weights[f_own : 2 * f_own, :], preferred_element_type=f32),
        )
        return carry

    lax.fori_loop(0, tiles, step, 0)

    for k, (left, right) in enumerate(((grad_gate, normed), (grad_up, normed), (act, upstream))):
        cut = slice(k * f_own, (k + 1) * f_own)
        for z in range(n_dp):
            pair = dot_tn(left[...], right[:, 2 * z * lane : (2 * z + 2) * lane])
            even = pair[:, :lane]
            odd = pair[:, lane:]
            kept_grads[z, cut, :] = jnp.where(ctx_first, even, odd).astype(bf16)
            given_grads[z, cut, :] = jnp.where(ctx_first, odd, even).astype(bf16)


def ffn_kernel(at, normed_own, normed_other, up_own, up_other, w_own, w_other, n_hi):
    n_dp, f_three, lane = w_own.shape
    rows, half = normed_own.shape
    parts = jax.ShapeDtypeStruct((n_dp, n_hi, 2, rows // n_dp, half // n_hi), bf16)
    grads = jax.ShapeDtypeStruct(w_own.shape, bf16)
    vmem = pl.BlockSpec(memory_space=pltpu.VMEM)
    hidden = pltpu.VMEM((rows, f_three // 3), bf16)
    return pl.pallas_call(
        ffn_body,
        out_shape=(parts, parts, grads, grads),
        in_specs=[pl.BlockSpec(memory_space=pltpu.SMEM)] + [vmem] * 6,
        out_specs=[vmem] * 4,
        scratch_shapes=[
            pltpu.VMEM((rows, 2 * half), bf16),
            pltpu.VMEM((rows, 2 * half), bf16),
            pltpu.VMEM((f_three, 2 * n_dp * lane), bf16),
            hidden,
            hidden,
            hidden,
        ],
        compiler_params=pltpu.CompilerParams(vmem_limit_bytes=48 * 1024 * 1024),
        name="ffn",
    )(at, normed_own, normed_other, up_own, up_other, w_own, w_other)


def per_device(
    tokens,
    cotangent,
    doc_lengths,
    norm1_gain,
    in_weight,
    conv_weight,
    out_weight,
    norm2_gain,
    gate_up_weight,
    down_weight,
    first_norm1,
    first_in,
    first_conv,
    first_out,
    first_norm2,
    first_gate_up,
    first_down,
    second_norm1,
    second_in,
    second_conv,
    second_out,
    second_norm2,
    second_gate_up,
    second_down,
):
    n_dp = lax.axis_size("dp")
    n_ctx = lax.axis_size("ctx")
    n_hi = lax.axis_size("hi")
    n_lo = lax.axis_size("lo")
    n_tp = n_hi * n_lo
    n_data = n_dp * n_ctx
    at_ctx = lax.axis_index("ctx")
    at_lo = lax.axis_index("lo")

    rows = tokens.reshape(-1, tokens.shape[-1])
    upstream_f = cotangent.reshape(rows.shape)
    count, width = rows.shape
    length = count * n_ctx
    d_own = in_weight.shape[1]
    c_tp = in_weight.shape[2]
    c_own = c_tp // n_ctx
    f_tp = down_weight.shape[0]
    f_own = f_tp // n_dp
    half = width // n_lo
    quarter = width // n_tp

    mixer_own = jnp.concatenate([in_weight, out_weight.T[None]]).astype(bf16)
    mixer_own = mixer_own.reshape(4, d_own, n_ctx, c_own).transpose(2, 0, 1, 3)
    mixer_own = mixer_own.reshape(n_ctx, 4 * d_own, c_own)
    gains = jnp.concatenate([norm1_gain, norm2_gain]).astype(bf16)
    gains = jnp.pad(gains, (0, -gains.shape[0] % c_own)).reshape(-1, c_own)
    gains = jnp.broadcast_to(gains[None], (n_ctx, *gains.shape))
    mixer_own = jnp.concatenate([mixer_own, gains], axis=1)
    mixer_own = jnp.broadcast_to(mixer_own[None], (n_dp, *mixer_own.shape))
    mixer_all = exchange(mixer_own.reshape(n_data, -1, c_own), DATA)

    scale_one = rms_scale(rows)
    unit_one = rows * scale_one
    unit_seq = gather(unit_one.astype(bf16), "ctx").reshape(length, width)

    def half_rows(block):
        part = lax.dynamic_slice_in_dim(block, at_lo * half, half, 1)
        return jnp.broadcast_to(part[None], (n_dp, *part.shape))

    ffn_own = jnp.concatenate(
        [gate_up_weight.astype(bf16).transpose(0, 2, 1), down_weight.astype(bf16)[None]]
    )
    ffn_own = ffn_own.reshape(3, n_dp, f_own, d_own).transpose(1, 0, 2, 3)
    ffn_own = ffn_own.reshape(n_dp, 3 * f_own, d_own)
    up_own = half_rows(upstream_f.astype(bf16))
    mixer_all, ffn_own, up_own = lax.optimization_barrier((mixer_all, ffn_own, up_own))
    ffn_own = exchange(ffn_own, "dp")
    up_own = exchange(up_own, "dp").reshape(n_dp * count, half)

    w_mixer = mixer_all[:, : 4 * d_own].reshape(n_data, 4, d_own, c_own).transpose(1, 0, 2, 3)
    w_mixer = w_mixer.reshape(4, width, c_own)
    w_in = w_mixer[:3]
    w_out = w_mixer[3]
    gains_all = mixer_all[:, 4 * d_own :].reshape(n_data, -1).astype(f32)
    gain_one = gains_all[:, :d_own].reshape(width)
    gain_two = gains_all[:, d_own : 2 * d_own].reshape(width)
    normed_seq = (unit_seq.astype(f32) * gain_one).astype(bf16)

    mask_one, mask_two = doc_masks(doc_lengths[0], length + 2)
    taps = lax.dynamic_slice_in_dim(conv_weight, at_ctx * c_own, c_own, 1)
    projected = jnp.einsum("td,kdc->ktc", normed_seq, w_in, preferred_element_type=f32)
    gate_b = projected[0]
    gate_c = projected[1]
    values_x = projected[2]
    mixed_in = gate_b * values_x
    extended = jnp.pad(mixed_in, ((2, 0), (0, 0)))
    lag_one = extended[1 : length + 1] * mask_one[:length]
    lag_two = extended[:length] * mask_two[:length]
    conv_out = taps[0] * lag_two + taps[1] * lag_one + taps[2] * mixed_in
    gated_y = (gate_c * conv_out).astype(bf16)

    def mixer_sum(part):
        blocks = part.astype(bf16).reshape(n_ctx, count, n_tp, quarter).transpose(0, 2, 1, 3)
        blocks = exchange(blocks.reshape(n_ctx * n_tp, count, quarter), ("ctx", *MODEL))
        return jnp.sum(blocks.astype(f32), axis=0)

    mixer_part = dot_nt(gated_y, w_out)
    mixer_out = gather_features(mixer_sum(mixer_part).astype(bf16)).astype(f32)
    hidden_rows = rows + mixer_out
    scale_two = rms_scale(hidden_rows)
    unit_two = hidden_rows * scale_two
    normed_two = half_rows((unit_two * gain_two).astype(bf16))
    normed_own = exchange(normed_two, "dp").reshape(n_dp * count, half)
    if n_ctx == 2 and n_lo == 2 and d_own % 128 == 0 and f_own % 16 == 0:
        at = jnp.stack([at_ctx, at_lo])
        kept_rows, given_rows, kept_grads, given_grads = ffn_kernel(
            at,
            normed_own,
            swap(normed_own, "lo"),
            up_own,
            swap(up_own, "lo"),
            ffn_own,
            swap(ffn_own, "ctx"),
            n_hi,
        )
        parts = kept_rows.astype(f32) + swap(given_rows, "lo").astype(f32)
        parts = parts.astype(bf16).reshape(n_dp * n_hi, 2, count, quarter)
        grad_ffn = kept_grads.astype(f32) + swap(given_grads, "ctx").astype(f32)
    else:
        normed_two = gather_last(normed_own, "lo")
        upstream = gather_last(up_own, "lo")
        w_ffn = gather(ffn_own, "ctx").reshape(n_ctx, n_dp, 3, f_own, d_own)
        w_ffn = w_ffn.transpose(2, 3, 1, 0, 4).reshape(3, f_own, width)
        w_gate_up = w_ffn[:2]
        w_down = w_ffn[2]
        gate_up = jnp.einsum("td,kfd->ktf", normed_two, w_gate_up, preferred_element_type=f32)
        gate_pre = gate_up[0]
        up_pre = gate_up[1]
        sig = jax.nn.sigmoid(gate_pre)
        activated = (gate_pre * sig * up_pre).astype(bf16)
        grad_act = dot_nt(upstream, w_down)
        grad_gate = (grad_act * up_pre * sig * (1.0 + gate_pre * (1.0 - sig))).astype(bf16)
        grad_up = (grad_act * gate_pre * sig).astype(bf16)
        both = jnp.stack([grad_gate, grad_up])
        ffn_part = jnp.dot(activated, w_down, preferred_element_type=f32)
        normed_part = jnp.einsum("ktf,kfd->td", both, w_gate_up, preferred_element_type=f32)
        parts = jnp.stack([ffn_part.astype(bf16), normed_part.astype(bf16)])
        parts = parts.reshape(2, n_dp * count, n_lo, half).transpose(2, 0, 1, 3)
        parts = sum_scatter(parts, "lo").astype(bf16)
        parts = parts.reshape(2, n_dp, count, n_hi, quarter).transpose(1, 3, 0, 2, 4)
        parts = parts.reshape(n_dp * n_hi, 2, count, quarter)
        grad_gate_up = jnp.einsum("ktf,td->kfd", both, normed_two, preferred_element_type=f32)
        grad_down = dot_tn(activated, upstream)
        grad_ffn = jnp.concatenate([grad_gate_up.astype(bf16), grad_down.astype(bf16)[None]])
        grad_ffn = grad_ffn.reshape(3 * f_own, n_dp, n_ctx, d_own).transpose(2, 1, 0, 3)
        grad_ffn = sum_scatter(grad_ffn, "ctx")

    parts = exchange(parts, ("dp", "hi"))
    parts = jnp.sum(parts.astype(f32), axis=0).astype(bf16)
    parts = gather_features(parts).astype(f32)
    result = hidden_rows + parts[0]
    grad_normed_two = parts[1]

    grad_norm2 = jnp.sum(grad_normed_two * unit_two, axis=0)
    grad_hidden = upstream_f + norm_back(grad_normed_two, unit_two, gain_two, scale_two)
    grad_hidden_b = grad_hidden.astype(bf16)
    grad_hidden_b, grad_ffn = lax.optimization_barrier((grad_hidden_b, grad_ffn.astype(bf16)))
    grad_seq = gather(grad_hidden_b, "ctx").reshape(length, width)
    grad_ffn = exchange(grad_ffn, "dp").reshape(n_dp, 3, f_own, d_own).transpose(1, 0, 2, 3)
    grad_ffn = grad_ffn.reshape(3, f_tp, d_own)
    owned_gate_up = row_major(grad_ffn[:2].transpose(0, 2, 1)).astype(f32)
    owned_down = grad_ffn[2].astype(f32)

    grad_y = jnp.dot(grad_seq, w_out, preferred_element_type=f32)
    grad_out = dot_tn(grad_seq, gated_y)
    grad_c = grad_y * conv_out
    grad_conv_in = grad_y * gate_c
    grad_ext = jnp.pad(grad_conv_in, ((0, 2), (0, 0)))
    lead_one = (grad_ext * mask_one)[1 : length + 1]
    lead_two = (grad_ext * mask_two)[2:]
    grad_mixed = taps[2] * grad_conv_in + taps[1] * lead_one + taps[0] * lead_two
    grad_taps = jnp.stack(
        [
            jnp.sum(grad_conv_in * lag_two, axis=0),
            jnp.sum(grad_conv_in * lag_one, axis=0),
            jnp.sum(grad_conv_in * mixed_in, axis=0),
        ]
    )
    grad_gates = jnp.stack(
        [
            (grad_mixed * values_x).astype(bf16),
            grad_c.astype(bf16),
            (grad_mixed * gate_b).astype(bf16),
        ]
    )
    normed_one_part = jnp.einsum("ktc,kdc->td", grad_gates, w_in, preferred_element_type=f32)
    grad_normed_one = gather_features(mixer_sum(normed_one_part).astype(bf16)).astype(f32)
    grad_norm1 = jnp.sum(grad_normed_one * unit_one, axis=0)
    grad_tokens = grad_hidden + norm_back(grad_normed_one, unit_one, gain_one, scale_one)

    grad_in = jnp.einsum("td,ktc->kdc", normed_seq, grad_gates, preferred_element_type=f32)
    grad_mixer = jnp.concatenate([grad_in.astype(bf16), grad_out.astype(bf16)[None]])
    grad_mixer = grad_mixer.reshape(4, n_data, d_own, c_own).transpose(1, 0, 2, 3)
    grad_mixer = grad_mixer.reshape(n_data, 4 * d_own, c_own)
    small = jnp.concatenate(
        [
            grad_norm1.reshape(n_data, d_own),
            grad_norm2.reshape(n_data, d_own),
            jnp.broadcast_to(grad_taps.reshape(1, -1), (n_data, grad_taps.size)),
        ],
        axis=1,
    ).astype(bf16)
    n_small = small.shape[1]
    small = jnp.pad(small, ((0, 0), (0, -n_small % c_own))).reshape(n_data, -1, c_own)
    mixed = exchange(jnp.concatenate([grad_mixer, small], axis=1), DATA).astype(f32)
    mixed = mixed.reshape(n_dp, n_ctx, -1, c_own)
    owned_mixer = jnp.sum(mixed[:, :, : 4 * d_own], axis=0).reshape(n_ctx, 4, d_own, c_own)
    owned_mixer = owned_mixer.transpose(1, 2, 0, 3).reshape(4, d_own, c_tp)
    owned_in = owned_mixer[:3]
    owned_out = owned_mixer[3].T
    small = jnp.sum(mixed[:, :, 4 * d_own :], axis=0).reshape(n_ctx, -1)
    owned_norm1 = jnp.sum(small[:, :d_own], axis=0)
    owned_norm2 = jnp.sum(small[:, d_own : 2 * d_own], axis=0)
    grad_conv = small[:, 2 * d_own : n_small].reshape(n_ctx, 3, c_own)
    grad_conv = grad_conv.transpose(1, 0, 2).reshape(3, c_tp)

    steps = jnp.float32(STEP)
    bias_one = 1.0 - jnp.power(jnp.float32(BETA_ONE), steps)
    bias_two = 1.0 - jnp.power(jnp.float32(BETA_TWO), steps)
    new_norm1, new_first_norm1, new_second_norm1 = adamw(
        norm1_gain, owned_norm1, first_norm1, second_norm1, bias_one, bias_two
    )
    new_in, new_first_in, new_second_in = adamw(
        in_weight, owned_in, first_in, second_in, bias_one, bias_two
    )
    new_conv, new_first_conv, new_second_conv = adamw(
        conv_weight, grad_conv, first_conv, second_conv, bias_one, bias_two
    )
    new_out, new_first_out, new_second_out = adamw(
        out_weight, owned_out, first_out, second_out, bias_one, bias_two
    )
    new_norm2, new_first_norm2, new_second_norm2 = adamw(
        norm2_gain, owned_norm2, first_norm2, second_norm2, bias_one, bias_two
    )
    new_gate_up, new_first_gate_up, new_second_gate_up = adamw(
        gate_up_weight, owned_gate_up, first_gate_up, second_gate_up, bias_one, bias_two
    )
    new_down, new_first_down, new_second_down = adamw(
        down_weight, owned_down, first_down, second_down, bias_one, bias_two
    )
    return (
        result.reshape(tokens.shape),
        grad_tokens.reshape(tokens.shape),
        owned_norm1,
        owned_in,
        grad_conv,
        owned_out,
        owned_norm2,
        owned_gate_up,
        owned_down,
        new_norm1,
        new_in,
        new_conv,
        new_out,
        new_norm2,
        new_gate_up,
        new_down,
        new_first_norm1,
        new_first_in,
        new_first_conv,
        new_first_out,
        new_first_norm2,
        new_first_gate_up,
        new_first_down,
        new_second_norm1,
        new_second_in,
        new_second_conv,
        new_second_out,
        new_second_norm2,
        new_second_gate_up,
        new_second_down,
    )


def solution(mesh):
    n_dp, n_ctx, n_tp = (mesh.shape[name] for name in ("dp", "ctx", "tp"))
    n_lo = 2 if n_tp % 2 == 0 else 1
    devices = mesh.devices.reshape(n_dp, n_ctx, n_tp // n_lo, n_lo)
    paired = Mesh(devices, ("dp", "ctx", "hi", "lo"))
    tp = ("hi", "lo")

    row = P("dp", "ctx", None)
    params = (
        P(DATA),
        P(None, DATA, tp),
        P(None, tp),
        P(tp, DATA),
        P(DATA),
        P(None, DATA, tp),
        P(tp, DATA),
    )
    return jax.shard_map(
        per_device,
        mesh=paired,
        in_specs=(row, row, P("dp", None), *params, *params, *params),
        out_specs=(row, row, *params, *params, *params, *params),
        check_vma=False,
    )
```

```python
import functools

import jax
import jax.numpy as jnp
from jax import lax
from jax.experimental import pallas as pl
from jax.experimental.layout import Layout, with_layout_constraint
from jax.experimental.pallas import tpu as pltpu
from jax.sharding import Mesh, PartitionSpec as P

STEP = 5


EPS_NORM = 1e-05
BETA_ONE = 0.9
BETA_TWO = 0.95
LEARN_RATE = 0.01
DECAY_RATE = 0.1
ADAM_EPS = 1e-08

DATA = ("dp", "ctx")
MODEL = ("lo", "hi")


bf16 = jnp.bfloat16
f32 = jnp.float32


def doc_masks(lengths_row, count):
    positions = jnp.arange(count, dtype=jnp.int32)
    starts = jnp.cumsum(lengths_row) - lengths_row
    inside = starts[None, :] <= positions[:, None]
    doc_start = jnp.max(jnp.where(inside, starts[None, :], jnp.int32(0)), axis=1)
    mask_one = (positions - 1 >= doc_start).astype(f32)[:, None]
    mask_two = (positions - 2 >= doc_start).astype(f32)[:, None]
    return (mask_one, mask_two)


def rms_scale(inputs):
    return lax.rsqrt(jnp.mean(inputs * inputs, axis=-1, keepdims=True) + EPS_NORM)


def norm_back(grad_normed, unit_rows, gain_full, scale_rows):
    scaled = grad_normed * gain_full
    return scale_rows * (scaled - unit_rows * jnp.mean(scaled * unit_rows, axis=-1, keepdims=True))


def adamw(param, grads, first, second, bias_one, bias_two):
    new_first = BETA_ONE * first + (1.0 - BETA_ONE) * grads
    new_second = BETA_TWO * second + (1.0 - BETA_TWO) * grads * grads
    update = (
        new_first / bias_one / (jnp.sqrt(new_second / bias_two) + ADAM_EPS) + DECAY_RATE * param
    )
    return (param - LEARN_RATE * update, new_first, new_second)


def exchange(blocks, axes):
    return lax.all_to_all(blocks, axes, 0, 0, tiled=True)


def shift(block, k):
    n = lax.axis_size("dp")
    return lax.ppermute(block, "dp", [(i, (i + k) % n) for i in range(n)])


def fetch_all(block):
    return [block] + [shift(block, k) for k in range(1, lax.axis_size("dp"))]


def send_each(blocks):
    return [blocks[0]] + [shift(blocks[k], k) for k in range(1, lax.axis_size("dp"))]


def by_distance(blocks):
    n = lax.axis_size("dp")
    at = lax.axis_index("dp")
    return [lax.dynamic_index_in_dim(blocks, (at + k) % n, 0, keepdims=False) for k in range(n)]


def by_member(items):
    n = lax.axis_size("dp")
    at = lax.axis_index("dp")
    stacked = jnp.stack(items)
    return jnp.stack(
        [lax.dynamic_index_in_dim(stacked, (at - q) % n, 0, keepdims=False) for q in range(n)]
    )


def swap(block, axis):
    return lax.ppermute(block, axis, [(0, 1), (1, 0)])


def gather(block, axis):
    if lax.axis_size(axis) == 2:
        other = swap(block, axis)
        first = lax.axis_index(axis) == 0
        return jnp.stack([jnp.where(first, block, other), jnp.where(first, other, block)])
    return lax.all_gather(block, axis)


def sum_scatter(blocks, axis):
    if lax.axis_size(axis) == 2:
        mine = lax.axis_index(axis)
        kept = lax.dynamic_index_in_dim(blocks, mine, 0, keepdims=False)
        given = lax.dynamic_index_in_dim(blocks, 1 - mine, 0, keepdims=False)
        return kept.astype(f32) + swap(given, axis).astype(f32)
    return jnp.sum(exchange(blocks, axis).astype(f32), axis=0)


def gather_last(block, axis):
    if lax.axis_size(axis) == 2:
        other = swap(block, axis)
        first = lax.axis_index(axis) == 0
        return jnp.concatenate(
            [jnp.where(first, block, other), jnp.where(first, other, block)], axis=-1
        )
    return lax.all_gather(block, axis, axis=block.ndim - 1, tiled=True)


def gather_features(block):
    return gather_last(gather_last(block, "hi"), "lo")


def row_major(block):
    return with_layout_constraint(block, Layout(major_to_minor=tuple(range(block.ndim))))


def dot_nt(left, right):
    return lax.dot_general(left, right, (((1,), (1,)), ((), ())), preferred_element_type=f32)


def dot_tn(left, right):
    return lax.dot_general(left, right, (((0,), (0,)), ((), ())), preferred_element_type=f32)


def ffn_body(n_dp, at, *refs):
    normed_own, normed_other, up_own, up_other = refs[:4]
    w_own = refs[4 : 4 + n_dp]
    w_other = refs[4 + n_dp : 4 + 2 * n_dp]
    kept_ffn, given_ffn, kept_grad, given_grad, kept_w, given_w = refs[4 + 2 * n_dp : 10 + 2 * n_dp]
    normed, upstream, weights, act, grad_gate, grad_up = refs[10 + 2 * n_dp :]
    f_three, lane = w_own[0].shape
    f_own = f_three // 3
    rows, half = normed_own.shape
    count = rows // n_dp
    n_hi = kept_ffn.shape[1]
    quarter = half // n_hi
    ctx_first = at[0] == 0
    lo_first = at[1] == 0

    def member(k):
        return lax.rem(at[2] + (n_dp - k), n_dp)

    def place(even, odd):
        for k in range(n_dp):
            left = pl.multiple_of(member(k) * (2 * lane), 2 * lane)
            weights[:, pl.ds(left, lane)] = even[k][...]
            weights[:, pl.ds(pl.multiple_of(left + lane, lane), lane)] = odd[k][...]

    @pl.when(ctx_first)
    def _():
        place(w_own, w_other)

    @pl.when(jnp.logical_not(ctx_first))
    def _():
        place(w_other, w_own)

    @pl.when(lo_first)
    def _():
        normed[:, :half] = normed_own[...]
        normed[:, half:] = normed_other[...]
        upstream[:, :half] = up_own[...]
        upstream[:, half:] = up_other[...]

    @pl.when(jnp.logical_not(lo_first))
    def _():
        normed[:, :half] = normed_other[...]
        normed[:, half:] = normed_own[...]
        upstream[:, :half] = up_other[...]
        upstream[:, half:] = up_own[...]

    tiles = 2
    tile = rows // tiles

    def step(i, carry):
        part = pl.ds(pl.multiple_of(i * tile, tile), tile)
        n_rows = normed[part, :]
        gate_pre = dot_nt(n_rows, weights[:f_own, :])
        up_pre = dot_nt(n_rows, weights[f_own : 2 * f_own, :])
        grad_act = dot_nt(upstream[part, :], weights[2 * f_own :, :])
        sig = 1.0 / (1.0 + jnp.exp(-gate_pre))
        gated = gate_pre * sig
        act[part, :] = (gated * up_pre).astype(bf16)
        grad_gate[part, :] = (grad_act * up_pre * sig * (1.0 + gate_pre * (1.0 - sig))).astype(bf16)
        grad_up[part, :] = (grad_act * gated).astype(bf16)

        def send(kept_out, given_out, values):
            kept = jnp.where(lo_first, values[:, :half], values[:, half:]).astype(bf16)
            given = jnp.where(lo_first, values[:, half:], values[:, :half]).astype(bf16)
            for j in range(n_dp // tiles):
                z = member(i * (n_dp // tiles) + j)
                for h in range(n_hi):
                    cut = (slice(j * count, (j + 1) * count), slice(h * quarter, (h + 1) * quarter))
                    kept_out[z, h] = kept[cut]
                    given_out[z, h] = given[cut]

        send(
            kept_ffn,
            given_ffn,
            jnp.dot(act[part, :], weights[2 * f_own :, :], preferred_element_type=f32),
        )
        send(
            kept_grad,
            given_grad,
            jnp.dot(grad_gate[part, :], weights[:f_own, :], preferred_element_type=f32)
            + jnp.dot(grad_up[part, :], weights[f_own : 2 * f_own, :], preferred_element_type=f32),
        )
        return carry

    lax.fori_loop(0, tiles, step, 0)

    for k, (left, right) in enumerate(((grad_gate, normed), (grad_up, normed), (act, upstream))):
        cut = slice(k * f_own, (k + 1) * f_own)
        for z in range(n_dp):
            away = lax.rem(z + n_dp - at[2], n_dp)
            pair = dot_tn(left[...], right[:, 2 * z * lane : (2 * z + 2) * lane])
            even = pair[:, :lane]
            odd = pair[:, lane:]
            kept_w[away, cut, :] = jnp.where(ctx_first, even, odd).astype(bf16)
            given_w[away, cut, :] = jnp.where(ctx_first, odd, even).astype(bf16)


def ffn_kernel(at, normed_own, normed_other, up_own, up_other, w_own, w_other, n_hi):
    n_dp = len(w_own)
    f_three, lane = w_own[0].shape
    rows, half = normed_own.shape
    parts = jax.ShapeDtypeStruct((n_dp, n_hi, rows // n_dp, half // n_hi), bf16)
    grads = jax.ShapeDtypeStruct((n_dp, f_three, lane), bf16)
    vmem = pl.BlockSpec(memory_space=pltpu.VMEM)
    hidden = pltpu.VMEM((rows, f_three // 3), bf16)
    return pl.pallas_call(
        functools.partial(ffn_body, n_dp),
        out_shape=(parts, parts, parts, parts, grads, grads),
        in_specs=[pl.BlockSpec(memory_space=pltpu.SMEM)] + [vmem] * (4 + 2 * n_dp),
        out_specs=[vmem] * 6,
        scratch_shapes=[
            pltpu.VMEM((rows, 2 * half), bf16),
            pltpu.VMEM((rows, 2 * half), bf16),
            pltpu.VMEM((f_three, 2 * n_dp * lane), bf16),
            hidden,
            hidden,
            hidden,
        ],
        compiler_params=pltpu.CompilerParams(vmem_limit_bytes=48 * 1024 * 1024),
        name="ffn",
    )(at, normed_own, normed_other, up_own, up_other, *w_own, *w_other)


def per_device(
    tokens,
    cotangent,
    doc_lengths,
    norm1_gain,
    in_weight,
    conv_weight,
    out_weight,
    norm2_gain,
    gate_up_weight,
    down_weight,
    first_norm1,
    first_in,
    first_conv,
    first_out,
    first_norm2,
    first_gate_up,
    first_down,
    second_norm1,
    second_in,
    second_conv,
    second_out,
    second_norm2,
    second_gate_up,
    second_down,
):
    n_dp = lax.axis_size("dp")
    n_ctx = lax.axis_size("ctx")
    n_hi = lax.axis_size("hi")
    n_lo = lax.axis_size("lo")
    n_tp = n_hi * n_lo
    n_data = n_dp * n_ctx
    at_ctx = lax.axis_index("ctx")
    at_lo = lax.axis_index("lo")

    rows = tokens.reshape(-1, tokens.shape[-1])
    upstream_f = cotangent.reshape(rows.shape)
    count, width = rows.shape
    length = count * n_ctx
    d_own = in_weight.shape[1]
    c_tp = in_weight.shape[2]
    c_own = c_tp // n_ctx
    f_tp = down_weight.shape[0]
    f_own = f_tp // n_dp
    half = width // n_lo
    quarter = width // n_tp

    mixer_own = jnp.concatenate([in_weight, out_weight.T[None]]).astype(bf16)
    mixer_own = mixer_own.reshape(4, d_own, n_ctx, c_own).transpose(2, 0, 1, 3)
    mixer_own = mixer_own.reshape(n_ctx, 4 * d_own, c_own)
    gains = jnp.concatenate([norm1_gain, norm2_gain]).astype(bf16)
    gains = jnp.pad(gains, (0, -gains.shape[0] % c_own)).reshape(-1, c_own)
    gains = jnp.broadcast_to(gains[None], (n_ctx, *gains.shape))
    mixer_own = jnp.concatenate([mixer_own, gains], axis=1)
    mixer_own = jnp.broadcast_to(mixer_own[None], (n_dp, *mixer_own.shape))
    mixer_all = exchange(mixer_own.reshape(n_data, -1, c_own), DATA)

    scale_one = rms_scale(rows)
    unit_one = rows * scale_one
    unit_seq = gather(unit_one.astype(bf16), "ctx").reshape(length, width)

    def half_rows(block):
        return lax.dynamic_slice_in_dim(block, at_lo * half, half, 1)

    ffn_own = jnp.concatenate(
        [gate_up_weight.astype(bf16).transpose(0, 2, 1), down_weight.astype(bf16)[None]]
    )
    ffn_own = ffn_own.reshape(3, n_dp, f_own, d_own).transpose(1, 0, 2, 3)
    ffn_own = by_distance(ffn_own.reshape(n_dp, 3 * f_own, d_own))
    up_own = half_rows(upstream_f.astype(bf16))
    mixer_all, ffn_own, up_own = lax.optimization_barrier((mixer_all, ffn_own, up_own))
    ffn_own = send_each(ffn_own)
    up_own = jnp.concatenate(fetch_all(up_own))

    w_mixer = mixer_all[:, : 4 * d_own].reshape(n_data, 4, d_own, c_own).transpose(1, 0, 2, 3)
    w_mixer = w_mixer.reshape(4, width, c_own)
    w_in = w_mixer[:3]
    w_out = w_mixer[3]
    gains_all = mixer_all[:, 4 * d_own :].reshape(n_data, -1).astype(f32)
    gain_one = gains_all[:, :d_own].reshape(width)
    gain_two = gains_all[:, d_own : 2 * d_own].reshape(width)
    normed_seq = (unit_seq.astype(f32) * gain_one).astype(bf16)

    mask_one, mask_two = doc_masks(doc_lengths[0], length + 2)
    taps = lax.dynamic_slice_in_dim(conv_weight, at_ctx * c_own, c_own, 1)
    projected = jnp.einsum("td,kdc->ktc", normed_seq, w_in, preferred_element_type=f32)
    gate_b = projected[0]
    gate_c = projected[1]
    values_x = projected[2]
    mixed_in = gate_b * values_x
    extended = jnp.pad(mixed_in, ((2, 0), (0, 0)))
    lag_one = extended[1 : length + 1] * mask_one[:length]
    lag_two = extended[:length] * mask_two[:length]
    conv_out = taps[0] * lag_two + taps[1] * lag_one + taps[2] * mixed_in
    gated_y = (gate_c * conv_out).astype(bf16)

    def mixer_sum(part):
        blocks = part.astype(bf16).reshape(n_ctx, count, n_tp, quarter).transpose(0, 2, 1, 3)
        blocks = exchange(blocks.reshape(n_ctx * n_tp, count, quarter), ("ctx", *MODEL))
        return jnp.sum(blocks.astype(f32), axis=0)

    mixer_part = dot_nt(gated_y, w_out)
    mixer_out = gather_features(mixer_sum(mixer_part).astype(bf16)).astype(f32)
    hidden_rows = rows + mixer_out
    scale_two = rms_scale(hidden_rows)
    unit_two = hidden_rows * scale_two
    normed_own = jnp.concatenate(fetch_all(half_rows((unit_two * gain_two).astype(bf16))))
    if n_ctx == 2 and n_lo == 2 and n_dp % 2 == 0 and d_own % 128 == 0 and f_own % 16 == 0:
        kept_ffn, given_ffn, kept_grad, given_grad, kept_w, given_w = ffn_kernel(
            jnp.stack([at_ctx, at_lo, lax.axis_index("dp")]),
            normed_own,
            swap(normed_own, "lo"),
            up_own,
            swap(up_own, "lo"),
            ffn_own,
            [swap(block, "ctx") for block in ffn_own],
            n_hi,
        )
        grad_part = (kept_grad.astype(f32) + swap(given_grad, "lo").astype(f32)).astype(bf16)
        ffn_part = (kept_ffn.astype(f32) + swap(given_ffn, "lo").astype(f32)).astype(bf16)
        grad_part = grad_part.reshape(n_dp * n_hi, count, quarter)
        ffn_part = ffn_part.reshape(n_dp * n_hi, count, quarter)
        grad_ffn = (kept_w.astype(f32) + swap(given_w, "ctx").astype(f32)).astype(bf16)
        grad_ffn = [grad_ffn[k] for k in range(n_dp)]
    else:
        by_order = by_member(list(normed_own.reshape(n_dp, count, half)))
        normed_two = gather_last(by_order.reshape(n_dp * count, half), "lo")
        by_order = by_member(list(up_own.reshape(n_dp, count, half)))
        upstream = gather_last(by_order.reshape(n_dp * count, half), "lo")
        w_ffn = gather(by_member(ffn_own), "ctx").reshape(n_ctx, n_dp, 3, f_own, d_own)
        w_ffn = w_ffn.transpose(2, 3, 1, 0, 4).reshape(3, f_own, width)
        w_gate_up = w_ffn[:2]
        w_down = w_ffn[2]
        gate_up = jnp.einsum("td,kfd->ktf", normed_two, w_gate_up, preferred_element_type=f32)
        gate_pre = gate_up[0]
        up_pre = gate_up[1]
        sig = jax.nn.sigmoid(gate_pre)
        activated = (gate_pre * sig * up_pre).astype(bf16)
        grad_act = dot_nt(upstream, w_down)
        grad_gate = (grad_act * up_pre * sig * (1.0 + gate_pre * (1.0 - sig))).astype(bf16)
        grad_up = (grad_act * gate_pre * sig).astype(bf16)
        both = jnp.stack([grad_gate, grad_up])

        def sum_pairs(part):
            part = part.astype(bf16).reshape(n_dp * count, n_lo, half).transpose(1, 0, 2)
            part = sum_scatter(part, "lo").astype(bf16)
            part = part.reshape(n_dp, count, n_hi, quarter).transpose(0, 2, 1, 3)
            return part.reshape(n_dp * n_hi, count, quarter)

        ffn_part = sum_pairs(jnp.dot(activated, w_down, preferred_element_type=f32))
        grad_part = sum_pairs(
            jnp.einsum("ktf,kfd->td", both, w_gate_up, preferred_element_type=f32)
        )
        grad_gate_up = jnp.einsum("ktf,td->kfd", both, normed_two, preferred_element_type=f32)
        grad_down = dot_tn(activated, upstream)
        grad_ffn = jnp.concatenate([grad_gate_up.astype(bf16), grad_down.astype(bf16)[None]])
        grad_ffn = grad_ffn.reshape(3 * f_own, n_dp, n_ctx, d_own).transpose(2, 1, 0, 3)
        grad_ffn = by_distance(sum_scatter(grad_ffn, "ctx").astype(bf16))

    grad_part = exchange(grad_part, ("dp", "hi"))
    grad_part, ffn_part, grad_ffn = lax.optimization_barrier((grad_part, ffn_part, grad_ffn))
    grad_ffn = send_each(grad_ffn)
    grad_part = jnp.sum(grad_part.astype(f32), axis=0).astype(bf16)
    grad_normed_two = gather_features(grad_part).astype(f32)

    ffn_part = jnp.sum(exchange(ffn_part, ("dp", "hi")).astype(f32), axis=0).astype(bf16)
    result = hidden_rows + gather_features(ffn_part).astype(f32)

    grad_ffn = by_member(grad_ffn).reshape(n_dp, 3, f_own, d_own).transpose(1, 0, 2, 3)
    grad_ffn = grad_ffn.reshape(3, f_tp, d_own)
    owned_gate_up = row_major(grad_ffn[:2].transpose(0, 2, 1)).astype(f32)
    owned_down = grad_ffn[2].astype(f32)

    grad_norm2 = jnp.sum(grad_normed_two * unit_two, axis=0)
    grad_hidden = upstream_f + norm_back(grad_normed_two, unit_two, gain_two, scale_two)
    grad_seq = gather(grad_hidden.astype(bf16), "ctx").reshape(length, width)

    grad_y = jnp.dot(grad_seq, w_out, preferred_element_type=f32)
    grad_out = dot_tn(grad_seq, gated_y)
    grad_c = grad_y * conv_out
    grad_conv_in = grad_y * gate_c
    grad_ext = jnp.pad(grad_conv_in, ((0, 2), (0, 0)))
    lead_one = (grad_ext * mask_one)[1 : length + 1]
    lead_two = (grad_ext * mask_two)[2:]
    grad_mixed = taps[2] * grad_conv_in + taps[1] * lead_one + taps[0] * lead_two
    grad_taps = jnp.stack(
        [
            jnp.sum(grad_conv_in * lag_two, axis=0),
            jnp.sum(grad_conv_in * lag_one, axis=0),
            jnp.sum(grad_conv_in * mixed_in, axis=0),
        ]
    )
    grad_gates = jnp.stack(
        [
            (grad_mixed * values_x).astype(bf16),
            grad_c.astype(bf16),
            (grad_mixed * gate_b).astype(bf16),
        ]
    )
    grad_in = jnp.einsum("td,ktc->kdc", normed_seq, grad_gates, preferred_element_type=f32)
    grad_mixer = jnp.concatenate([grad_in.astype(bf16), grad_out.astype(bf16)[None]])
    grad_mixer = grad_mixer.reshape(4, n_dp, n_ctx, d_own, c_own).transpose(1, 2, 0, 3, 4)
    grad_mixer = send_each(by_distance(grad_mixer.reshape(n_dp, n_ctx, 4 * d_own, c_own)))
    grad_mixer = functools.reduce(jnp.add, [block.astype(f32) for block in grad_mixer])
    if n_ctx == 2:
        kept = lax.dynamic_index_in_dim(grad_mixer, at_ctx, 0, keepdims=False)
        given = lax.dynamic_index_in_dim(grad_mixer, 1 - at_ctx, 0, keepdims=False)
        other = swap(given.astype(bf16), "ctx").astype(f32)
        first = at_ctx == 0
        owned_mixer = jnp.stack([jnp.where(first, kept, other), jnp.where(first, other, kept)])
    else:
        owned_mixer = exchange(grad_mixer.astype(bf16), "ctx").astype(f32)
    owned_mixer = owned_mixer.reshape(n_ctx, 4, d_own, c_own).transpose(1, 2, 0, 3)
    owned_mixer = owned_mixer.reshape(4, d_own, c_tp)
    owned_in = owned_mixer[:3]
    owned_out = row_major(owned_mixer[3].T)

    normed_one_part = jnp.einsum("ktc,kdc->td", grad_gates, w_in, preferred_element_type=f32)
    grad_normed_one = gather_features(mixer_sum(normed_one_part).astype(bf16)).astype(f32)
    grad_norm1 = jnp.sum(grad_normed_one * unit_one, axis=0)
    grad_tokens = grad_hidden + norm_back(grad_normed_one, unit_one, gain_one, scale_one)

    small = jnp.concatenate(
        [
            grad_norm1.reshape(n_data, d_own),
            grad_norm2.reshape(n_data, d_own),
            jnp.broadcast_to(grad_taps.reshape(1, -1), (n_data, grad_taps.size)),
        ],
        axis=1,
    )
    small = jnp.sum(exchange(small, DATA).reshape(n_dp, n_ctx, -1), axis=0)
    owned_norm1 = jnp.sum(small[:, :d_own], axis=0)
    owned_norm2 = jnp.sum(small[:, d_own : 2 * d_own], axis=0)
    grad_conv = small[:, 2 * d_own :].reshape(n_ctx, 3, c_own)
    grad_conv = grad_conv.transpose(1, 0, 2).reshape(3, c_tp)

    steps = jnp.float32(STEP)
    bias_one = 1.0 - jnp.power(jnp.float32(BETA_ONE), steps)
    bias_two = 1.0 - jnp.power(jnp.float32(BETA_TWO), steps)
    new_norm1, new_first_norm1, new_second_norm1 = adamw(
        norm1_gain, owned_norm1, first_norm1, second_norm1, bias_one, bias_two
    )
    new_in, new_first_in, new_second_in = adamw(
        in_weight, owned_in, first_in, second_in, bias_one, bias_two
    )
    new_conv, new_first_conv, new_second_conv = adamw(
        conv_weight, grad_conv, first_conv, second_conv, bias_one, bias_two
    )
    new_out, new_first_out, new_second_out = adamw(
        out_weight, owned_out, first_out, second_out, bias_one, bias_two
    )
    new_norm2, new_first_norm2, new_second_norm2 = adamw(
        norm2_gain, owned_norm2, first_norm2, second_norm2, bias_one, bias_two
    )
    new_gate_up, new_first_gate_up, new_second_gate_up = adamw(
        gate_up_weight, owned_gate_up, first_gate_up, second_gate_up, bias_one, bias_two
    )
    new_down, new_first_down, new_second_down = adamw(
        down_weight, owned_down, first_down, second_down, bias_one, bias_two
    )
    return (
        result.reshape(tokens.shape),
        grad_tokens.reshape(tokens.shape),
        owned_norm1,
        owned_in,
        grad_conv,
        owned_out,
        owned_norm2,
        owned_gate_up,
        owned_down,
        new_norm1,
        new_in,
        new_conv,
        new_out,
        new_norm2,
        new_gate_up,
        new_down,
        new_first_norm1,
        new_first_in,
        new_first_conv,
        new_first_out,
        new_first_norm2,
        new_first_gate_up,
        new_first_down,
        new_second_norm1,
        new_second_in,
        new_second_conv,
        new_second_out,
        new_second_norm2,
        new_second_gate_up,
        new_second_down,
    )


def solution(mesh):
    n_dp, n_ctx, n_tp = (mesh.shape[name] for name in ("dp", "ctx", "tp"))
    n_lo = 2 if n_tp % 2 == 0 else 1
    devices = mesh.devices.reshape(n_dp, n_ctx, n_tp // n_lo, n_lo)
    paired = Mesh(devices, ("dp", "ctx", "hi", "lo"))
    tp = ("hi", "lo")

    row = P("dp", "ctx", None)
    params = (
        P(DATA),
        P(None, DATA, tp),
        P(None, tp),
        P(tp, DATA),
        P(DATA),
        P(None, DATA, tp),
        P(tp, DATA),
    )
    return jax.shard_map(
        per_device,
        mesh=paired,
        in_specs=(row, row, P("dp", None), *params, *params, *params),
        out_specs=(row, row, *params, *params, *params, *params),
        check_vma=False,
    )
```

```python
import functools

import jax
import jax.numpy as jnp
from jax import lax
from jax.experimental import pallas as pl
from jax.experimental.layout import Layout, with_layout_constraint
from jax.experimental.pallas import tpu as pltpu
from jax.sharding import Mesh, PartitionSpec as P


STEP = 5


EPS_NORM = 1e-05
BETA_ONE = 0.9
BETA_TWO = 0.95
LEARN_RATE = 0.01
DECAY_RATE = 0.1
ADAM_EPS = 1e-08

DATA = ("dp", "ctx")
MODEL = ("lo", "hi")


bf16 = jnp.bfloat16
f32 = jnp.float32


def doc_masks(lengths_row, count):
    positions = jnp.arange(count, dtype=jnp.int32)
    starts = jnp.cumsum(lengths_row) - lengths_row
    inside = starts[None, :] <= positions[:, None]
    doc_start = jnp.max(jnp.where(inside, starts[None, :], jnp.int32(0)), axis=1)
    mask_one = (positions - 1 >= doc_start).astype(f32)[:, None]
    mask_two = (positions - 2 >= doc_start).astype(f32)[:, None]
    return (mask_one, mask_two)


def rms_scale(inputs):
    return lax.rsqrt(jnp.mean(inputs * inputs, axis=-1, keepdims=True) + EPS_NORM)


def norm_back(grad_normed, unit_rows, gain_full, scale_rows):
    scaled = grad_normed * gain_full
    return scale_rows * (scaled - unit_rows * jnp.mean(scaled * unit_rows, axis=-1, keepdims=True))


def adamw(param, grads, first, second, bias_one, bias_two):
    new_first = BETA_ONE * first + (1.0 - BETA_ONE) * grads
    new_second = BETA_TWO * second + (1.0 - BETA_TWO) * grads * grads
    update = (
        new_first / bias_one / (jnp.sqrt(new_second / bias_two) + ADAM_EPS) + DECAY_RATE * param
    )
    return (param - LEARN_RATE * update, new_first, new_second)


def exchange(blocks, axes):
    return lax.all_to_all(blocks, axes, 0, 0, tiled=True)


def shift(block, k):
    n = lax.axis_size("dp")
    return lax.ppermute(block, "dp", [(i, (i + k) % n) for i in range(n)])


def fetch_all(block):
    return [block] + [shift(block, k) for k in range(1, lax.axis_size("dp"))]


def send_each(blocks):
    return [blocks[0]] + [shift(blocks[k], k) for k in range(1, lax.axis_size("dp"))]


def by_distance(blocks):
    n = lax.axis_size("dp")
    at = lax.axis_index("dp")
    return [lax.dynamic_index_in_dim(blocks, (at + k) % n, 0, keepdims=False) for k in range(n)]


def by_member(items):
    n = lax.axis_size("dp")
    at = lax.axis_index("dp")
    stacked = jnp.stack(items)
    return jnp.stack(
        [lax.dynamic_index_in_dim(stacked, (at - q) % n, 0, keepdims=False) for q in range(n)]
    )


def swap(block, axis):
    return lax.ppermute(block, axis, [(0, 1), (1, 0)])


def gather(block, axis):
    if lax.axis_size(axis) == 2:
        other = swap(block, axis)
        first = lax.axis_index(axis) == 0
        return jnp.stack([jnp.where(first, block, other), jnp.where(first, other, block)])
    return lax.all_gather(block, axis)


def sum_scatter(blocks, axis):
    if lax.axis_size(axis) == 2:
        mine = lax.axis_index(axis)
        kept = lax.dynamic_index_in_dim(blocks, mine, 0, keepdims=False)
        given = lax.dynamic_index_in_dim(blocks, 1 - mine, 0, keepdims=False)
        return kept.astype(f32) + swap(given, axis).astype(f32)
    return jnp.sum(exchange(blocks, axis).astype(f32), axis=0)


def gather_last(block, axis):
    if lax.axis_size(axis) == 2:
        other = swap(block, axis)
        first = lax.axis_index(axis) == 0
        return jnp.concatenate(
            [jnp.where(first, block, other), jnp.where(first, other, block)], axis=-1
        )
    return lax.all_gather(block, axis, axis=block.ndim - 1, tiled=True)


def gather_features(block):
    return gather_last(gather_last(block, "hi"), "lo")


def row_major(block):
    return with_layout_constraint(block, Layout(major_to_minor=tuple(range(block.ndim))))


def dot_nt(left, right):
    return lax.dot_general(left, right, (((1,), (1,)), ((), ())), preferred_element_type=f32)


def dot_tn(left, right):
    return lax.dot_general(left, right, (((0,), (0,)), ((), ())), preferred_element_type=f32)


def ffn_body(n_dp, at, *refs):
    normed_own, normed_other, up_own, up_other = refs[:4]
    w_own = refs[4 : 4 + n_dp]
    w_other = refs[4 + n_dp : 4 + 2 * n_dp]
    kept_ffn, given_ffn, kept_grad, given_grad, kept_w, given_w = refs[4 + 2 * n_dp : 10 + 2 * n_dp]
    normed, upstream, weights, act, grad_gate, grad_up = refs[10 + 2 * n_dp :]
    f_three, lane = w_own[0].shape
    f_own = f_three // 3
    rows, half = normed_own.shape
    count = rows // n_dp
    n_hi = kept_ffn.shape[1]
    quarter = half // n_hi
    ctx_first = at[0] == 0
    lo_first = at[1] == 0

    def member(k):
        return lax.rem(at[2] + (n_dp - k), n_dp)

    def place(even, odd):
        for k in range(n_dp):
            left = pl.multiple_of(member(k) * (2 * lane), 2 * lane)
            weights[:, pl.ds(left, lane)] = even[k][...]
            weights[:, pl.ds(pl.multiple_of(left + lane, lane), lane)] = odd[k][...]

    @pl.when(ctx_first)
    def _():
        place(w_own, w_other)

    @pl.when(jnp.logical_not(ctx_first))
    def _():
        place(w_other, w_own)

    @pl.when(lo_first)
    def _():
        normed[:, :half] = normed_own[...]
        normed[:, half:] = normed_other[...]
        upstream[:, :half] = up_own[...]
        upstream[:, half:] = up_other[...]

    @pl.when(jnp.logical_not(lo_first))
    def _():
        normed[:, :half] = normed_other[...]
        normed[:, half:] = normed_own[...]
        upstream[:, :half] = up_other[...]
        upstream[:, half:] = up_own[...]

    tiles = 2
    tile = rows // tiles

    def step(i, carry):
        part = pl.ds(pl.multiple_of(i * tile, tile), tile)
        n_rows = normed[part, :]
        gate_pre = dot_nt(n_rows, weights[:f_own, :])
        up_pre = dot_nt(n_rows, weights[f_own : 2 * f_own, :])
        grad_act = dot_nt(upstream[part, :], weights[2 * f_own :, :])
        sig = 1.0 / (1.0 + jnp.exp(-gate_pre))
        gated = gate_pre * sig
        act[part, :] = (gated * up_pre).astype(bf16)
        grad_gate[part, :] = (grad_act * up_pre * sig * (1.0 + gate_pre * (1.0 - sig))).astype(bf16)
        grad_up[part, :] = (grad_act * gated).astype(bf16)

        def send(kept_out, given_out, values):
            kept = jnp.where(lo_first, values[:, :half], values[:, half:]).astype(bf16)
            given = jnp.where(lo_first, values[:, half:], values[:, :half]).astype(bf16)
            for j in range(n_dp // tiles):
                z = member(i * (n_dp // tiles) + j)
                for h in range(n_hi):
                    cut = (slice(j * count, (j + 1) * count), slice(h * quarter, (h + 1) * quarter))
                    kept_out[z, h] = kept[cut]
                    given_out[z, h] = given[cut]

        send(
            kept_ffn,
            given_ffn,
            jnp.dot(act[part, :], weights[2 * f_own :, :], preferred_element_type=f32),
        )
        send(
            kept_grad,
            given_grad,
            jnp.dot(grad_gate[part, :], weights[:f_own, :], preferred_element_type=f32)
            + jnp.dot(grad_up[part, :], weights[f_own : 2 * f_own, :], preferred_element_type=f32),
        )
        return carry

    lax.fori_loop(0, tiles, step, 0)

    for k, (left, right) in enumerate(((grad_gate, normed), (grad_up, normed), (act, upstream))):
        cut = slice(k * f_own, (k + 1) * f_own)
        for z in range(n_dp):
            away = lax.rem(z + n_dp - at[2], n_dp)
            pair = dot_tn(left[...], right[:, 2 * z * lane : (2 * z + 2) * lane])
            even = pair[:, :lane]
            odd = pair[:, lane:]
            kept_w[away, cut, :] = jnp.where(ctx_first, even, odd).astype(bf16)
            given_w[away, cut, :] = jnp.where(ctx_first, odd, even).astype(bf16)


def ffn_kernel(at, normed_own, normed_other, up_own, up_other, w_own, w_other, n_hi):
    n_dp = len(w_own)
    f_three, lane = w_own[0].shape
    rows, half = normed_own.shape
    parts = jax.ShapeDtypeStruct((n_dp, n_hi, rows // n_dp, half // n_hi), bf16)
    grads = jax.ShapeDtypeStruct((n_dp, f_three, lane), bf16)
    vmem = pl.BlockSpec(memory_space=pltpu.VMEM)
    hidden = pltpu.VMEM((rows, f_three // 3), bf16)
    return pl.pallas_call(
        functools.partial(ffn_body, n_dp),
        out_shape=(parts, parts, parts, parts, grads, grads),
        in_specs=[pl.BlockSpec(memory_space=pltpu.SMEM)] + [vmem] * (4 + 2 * n_dp),
        out_specs=[vmem] * 6,
        scratch_shapes=[
            pltpu.VMEM((rows, 2 * half), bf16),
            pltpu.VMEM((rows, 2 * half), bf16),
            pltpu.VMEM((f_three, 2 * n_dp * lane), bf16),
            hidden,
            hidden,
            hidden,
        ],
        compiler_params=pltpu.CompilerParams(vmem_limit_bytes=48 * 1024 * 1024),
        name="ffn",
    )(at, normed_own, normed_other, up_own, up_other, *w_own, *w_other)


def per_device(
    tokens,
    cotangent,
    doc_lengths,
    norm1_gain,
    in_weight,
    conv_weight,
    out_weight,
    norm2_gain,
    gate_up_weight,
    down_weight,
    first_norm1,
    first_in,
    first_conv,
    first_out,
    first_norm2,
    first_gate_up,
    first_down,
    second_norm1,
    second_in,
    second_conv,
    second_out,
    second_norm2,
    second_gate_up,
    second_down,
):
    n_dp = lax.axis_size("dp")
    n_ctx = lax.axis_size("ctx")
    n_hi = lax.axis_size("hi")
    n_lo = lax.axis_size("lo")
    n_tp = n_hi * n_lo
    n_data = n_dp * n_ctx
    at_ctx = lax.axis_index("ctx")
    at_lo = lax.axis_index("lo")

    rows = tokens.reshape(-1, tokens.shape[-1])
    upstream_f = cotangent.reshape(rows.shape)
    count, width = rows.shape
    length = count * n_ctx
    d_own = in_weight.shape[1]
    c_tp = in_weight.shape[2]
    c_own = c_tp // n_ctx
    f_tp = down_weight.shape[0]
    f_own = f_tp // n_dp
    half = width // n_lo
    quarter = width // n_tp

    mixer_own = jnp.concatenate([in_weight, out_weight.T[None]]).astype(bf16)
    mixer_own = mixer_own.reshape(4, d_own, n_ctx, c_own).transpose(2, 0, 1, 3)
    mixer_own = mixer_own.reshape(n_ctx, 4 * d_own, c_own)
    gains = jnp.concatenate([norm1_gain, norm2_gain]).astype(bf16)
    gains = jnp.pad(gains, (0, -gains.shape[0] % c_own)).reshape(-1, c_own)
    gains = jnp.broadcast_to(gains[None], (n_ctx, *gains.shape))
    mixer_own = jnp.concatenate([mixer_own, gains], axis=1)
    mixer_own = jnp.broadcast_to(mixer_own[None], (n_dp, *mixer_own.shape))
    mixer_all = exchange(mixer_own.reshape(n_data, -1, c_own), DATA)

    scale_one = rms_scale(rows)
    unit_one = rows * scale_one
    unit_seq = gather(unit_one.astype(bf16), "ctx").reshape(length, width)

    def half_rows(block):
        return lax.dynamic_slice_in_dim(block, at_lo * half, half, 1)

    ffn_own = jnp.concatenate(
        [gate_up_weight.astype(bf16).transpose(0, 2, 1), down_weight.astype(bf16)[None]]
    )
    ffn_own = ffn_own.reshape(3, n_dp, f_own, d_own).transpose(1, 0, 2, 3)
    ffn_own = by_distance(ffn_own.reshape(n_dp, 3 * f_own, d_own))
    up_own = half_rows(upstream_f.astype(bf16))
    mixer_all, ffn_own, up_own = lax.optimization_barrier((mixer_all, ffn_own, up_own))
    ffn_own = send_each(ffn_own)
    up_own = jnp.concatenate(fetch_all(up_own))

    w_mixer = mixer_all[:, : 4 * d_own].reshape(n_data, 4, d_own, c_own).transpose(1, 0, 2, 3)
    w_mixer = w_mixer.reshape(4, width, c_own)
    w_in = w_mixer[:3]
    w_out = w_mixer[3]
    gains_all = mixer_all[:, 4 * d_own :].reshape(n_data, -1).astype(f32)
    gain_one = gains_all[:, :d_own].reshape(width)
    gain_two = gains_all[:, d_own : 2 * d_own].reshape(width)
    normed_seq = (unit_seq.astype(f32) * gain_one).astype(bf16)

    mask_one, mask_two = doc_masks(doc_lengths[0], length + 2)
    taps = lax.dynamic_slice_in_dim(conv_weight, at_ctx * c_own, c_own, 1)
    projected = jnp.einsum("td,kdc->ktc", normed_seq, w_in, preferred_element_type=f32)
    gate_b = projected[0]
    gate_c = projected[1]
    values_x = projected[2]
    mixed_in = gate_b * values_x
    extended = jnp.pad(mixed_in, ((2, 0), (0, 0)))
    lag_one = extended[1 : length + 1] * mask_one[:length]
    lag_two = extended[:length] * mask_two[:length]
    conv_out = taps[0] * lag_two + taps[1] * lag_one + taps[2] * mixed_in
    gated_y = (gate_c * conv_out).astype(bf16)

    def mixer_sum(part):
        blocks = part.astype(bf16).reshape(n_ctx, count, n_tp, quarter).transpose(0, 2, 1, 3)
        blocks = exchange(blocks.reshape(n_ctx * n_tp, count, quarter), ("ctx", *MODEL))
        return jnp.sum(blocks.astype(f32), axis=0)

    mixer_part = dot_nt(gated_y, w_out)
    mixer_out = gather_features(mixer_sum(mixer_part).astype(bf16)).astype(f32)
    hidden_rows = rows + mixer_out
    scale_two = rms_scale(hidden_rows)
    unit_two = hidden_rows * scale_two
    normed_own = jnp.concatenate(fetch_all(half_rows((unit_two * gain_two).astype(bf16))))
    if n_ctx == 2 and n_lo == 2 and n_dp % 2 == 0 and d_own % 128 == 0 and f_own % 16 == 0:
        normed_other = swap(normed_own, "lo")
        up_other = swap(up_own, "lo")
        ffn_other = [swap(block, "ctx") for block in ffn_own]
        kept_ffn, given_ffn, kept_grad, given_grad, kept_w, given_w = ffn_kernel(
            jnp.stack([at_ctx, at_lo, lax.axis_index("dp")]),
            normed_own,
            normed_other,
            up_own,
            up_other,
            ffn_own,
            ffn_other,
            n_hi,
        )
        grad_part = (kept_grad.astype(f32) + swap(given_grad, "lo").astype(f32)).astype(bf16)
        ffn_part = (kept_ffn.astype(f32) + swap(given_ffn, "lo").astype(f32)).astype(bf16)
        grad_part = grad_part.reshape(n_dp * n_hi, count, quarter)
        ffn_part = ffn_part.reshape(n_dp * n_hi, count, quarter)
        grad_ffn = (kept_w.astype(f32) + swap(given_w, "ctx").astype(f32)).astype(bf16)
        grad_ffn = [grad_ffn[k] for k in range(n_dp)]
    else:
        by_order = by_member(list(normed_own.reshape(n_dp, count, half)))
        normed_two = gather_last(by_order.reshape(n_dp * count, half), "lo")
        by_order = by_member(list(up_own.reshape(n_dp, count, half)))
        upstream = gather_last(by_order.reshape(n_dp * count, half), "lo")
        w_ffn = gather(by_member(ffn_own), "ctx").reshape(n_ctx, n_dp, 3, f_own, d_own)
        w_ffn = w_ffn.transpose(2, 3, 1, 0, 4).reshape(3, f_own, width)
        w_gate_up = w_ffn[:2]
        w_down = w_ffn[2]
        gate_up = jnp.einsum("td,kfd->ktf", normed_two, w_gate_up, preferred_element_type=f32)
        gate_pre = gate_up[0]
        up_pre = gate_up[1]
        sig = jax.nn.sigmoid(gate_pre)
        activated = (gate_pre * sig * up_pre).astype(bf16)
        grad_act = dot_nt(upstream, w_down)
        grad_gate = (grad_act * up_pre * sig * (1.0 + gate_pre * (1.0 - sig))).astype(bf16)
        grad_up = (grad_act * gate_pre * sig).astype(bf16)
        both = jnp.stack([grad_gate, grad_up])

        def sum_pairs(part):
            part = part.astype(bf16).reshape(n_dp * count, n_lo, half).transpose(1, 0, 2)
            part = sum_scatter(part, "lo").astype(bf16)
            part = part.reshape(n_dp, count, n_hi, quarter).transpose(0, 2, 1, 3)
            return part.reshape(n_dp * n_hi, count, quarter)

        ffn_part = sum_pairs(jnp.dot(activated, w_down, preferred_element_type=f32))
        grad_part = sum_pairs(
            jnp.einsum("ktf,kfd->td", both, w_gate_up, preferred_element_type=f32)
        )
        grad_gate_up = jnp.einsum("ktf,td->kfd", both, normed_two, preferred_element_type=f32)
        grad_down = dot_tn(activated, upstream)
        grad_ffn = jnp.concatenate([grad_gate_up.astype(bf16), grad_down.astype(bf16)[None]])
        grad_ffn = grad_ffn.reshape(3 * f_own, n_dp, n_ctx, d_own).transpose(2, 1, 0, 3)
        grad_ffn = by_distance(sum_scatter(grad_ffn, "ctx").astype(bf16))

    grad_part = exchange(grad_part, ("dp", "hi"))
    grad_part, ffn_part, grad_ffn = lax.optimization_barrier((grad_part, ffn_part, grad_ffn))
    grad_ffn = send_each(grad_ffn)
    grad_part = jnp.sum(grad_part.astype(f32), axis=0).astype(bf16)
    grad_normed_two = gather_features(grad_part).astype(f32)

    ffn_part = exchange(ffn_part, ("dp", "hi"))

    grad_norm2 = jnp.sum(grad_normed_two * unit_two, axis=0)
    grad_hidden = upstream_f + norm_back(grad_normed_two, unit_two, gain_two, scale_two)
    grad_seq = gather(grad_hidden.astype(bf16), "ctx").reshape(length, width)

    grad_y = jnp.dot(grad_seq, w_out, preferred_element_type=f32)
    grad_out = dot_tn(grad_seq, gated_y)
    grad_c = grad_y * conv_out
    grad_conv_in = grad_y * gate_c
    grad_ext = jnp.pad(grad_conv_in, ((0, 2), (0, 0)))
    lead_one = (grad_ext * mask_one)[1 : length + 1]
    lead_two = (grad_ext * mask_two)[2:]
    grad_mixed = taps[2] * grad_conv_in + taps[1] * lead_one + taps[0] * lead_two
    grad_taps = jnp.stack(
        [
            jnp.sum(grad_conv_in * lag_two, axis=0),
            jnp.sum(grad_conv_in * lag_one, axis=0),
            jnp.sum(grad_conv_in * mixed_in, axis=0),
        ]
    )
    grad_gates = jnp.stack(
        [
            (grad_mixed * values_x).astype(bf16),
            grad_c.astype(bf16),
            (grad_mixed * gate_b).astype(bf16),
        ]
    )
    ffn_part, grad_ffn, _ = lax.optimization_barrier((ffn_part, grad_ffn, grad_gates))
    ffn_part = jnp.sum(ffn_part.astype(f32), axis=0).astype(bf16)
    result = hidden_rows + gather_features(ffn_part).astype(f32)
    grad_ffn = by_member(grad_ffn).reshape(n_dp, 3, f_own, d_own).transpose(1, 0, 2, 3)
    grad_ffn = grad_ffn.reshape(3, f_tp, d_own)
    owned_gate_up = row_major(grad_ffn[:2].transpose(0, 2, 1)).astype(f32)
    owned_down = grad_ffn[2].astype(f32)

    grad_in = jnp.einsum("td,ktc->kdc", normed_seq, grad_gates, preferred_element_type=f32)
    grad_mixer = jnp.concatenate([grad_in.astype(bf16), grad_out.astype(bf16)[None]])
    grad_mixer = grad_mixer.reshape(4, n_dp, n_ctx, d_own, c_own).transpose(1, 2, 0, 3, 4)
    grad_mixer = by_distance(grad_mixer.reshape(n_dp, n_ctx, 4 * d_own, c_own))
    grad_mixer = send_each(grad_mixer)
    grad_mixer = functools.reduce(jnp.add, [block.astype(f32) for block in grad_mixer])
    if n_ctx == 2:
        kept = lax.dynamic_index_in_dim(grad_mixer, at_ctx, 0, keepdims=False)
        given = lax.dynamic_index_in_dim(grad_mixer, 1 - at_ctx, 0, keepdims=False)
        other = swap(given.astype(bf16), "ctx").astype(f32)
        first = at_ctx == 0
        owned_mixer = jnp.stack([jnp.where(first, kept, other), jnp.where(first, other, kept)])
    else:
        owned_mixer = exchange(grad_mixer.astype(bf16), "ctx").astype(f32)
    owned_mixer = owned_mixer.reshape(n_ctx, 4, d_own, c_own).transpose(1, 2, 0, 3)
    owned_mixer = owned_mixer.reshape(4, d_own, c_tp)
    owned_in = owned_mixer[:3]
    owned_out = row_major(owned_mixer[3].T)

    normed_one_part = jnp.einsum("ktc,kdc->td", grad_gates, w_in, preferred_element_type=f32)
    grad_normed_one = gather_features(mixer_sum(normed_one_part).astype(bf16))
    grad_normed_one = grad_normed_one.astype(f32)
    grad_norm1 = jnp.sum(grad_normed_one * unit_one, axis=0)
    grad_tokens = grad_hidden + norm_back(grad_normed_one, unit_one, gain_one, scale_one)

    small = jnp.concatenate(
        [
            grad_norm1.reshape(n_data, d_own),
            grad_norm2.reshape(n_data, d_own),
            jnp.broadcast_to(grad_taps.reshape(1, -1), (n_data, grad_taps.size)),
        ],
        axis=1,
    )
    small = exchange(small, DATA)
    small = jnp.sum(small.reshape(n_dp, n_ctx, -1), axis=0)
    owned_norm1 = jnp.sum(small[:, :d_own], axis=0)
    owned_norm2 = jnp.sum(small[:, d_own : 2 * d_own], axis=0)
    grad_conv = small[:, 2 * d_own :].reshape(n_ctx, 3, c_own)
    grad_conv = grad_conv.transpose(1, 0, 2).reshape(3, c_tp)

    steps = jnp.float32(STEP)
    bias_one = 1.0 - jnp.power(jnp.float32(BETA_ONE), steps)
    bias_two = 1.0 - jnp.power(jnp.float32(BETA_TWO), steps)
    new_norm1, new_first_norm1, new_second_norm1 = adamw(
        norm1_gain, owned_norm1, first_norm1, second_norm1, bias_one, bias_two
    )
    new_in, new_first_in, new_second_in = adamw(
        in_weight, owned_in, first_in, second_in, bias_one, bias_two
    )
    new_conv, new_first_conv, new_second_conv = adamw(
        conv_weight, grad_conv, first_conv, second_conv, bias_one, bias_two
    )
    new_out, new_first_out, new_second_out = adamw(
        out_weight, owned_out, first_out, second_out, bias_one, bias_two
    )
    new_norm2, new_first_norm2, new_second_norm2 = adamw(
        norm2_gain, owned_norm2, first_norm2, second_norm2, bias_one, bias_two
    )
    new_gate_up, new_first_gate_up, new_second_gate_up = adamw(
        gate_up_weight, owned_gate_up, first_gate_up, second_gate_up, bias_one, bias_two
    )
    new_down, new_first_down, new_second_down = adamw(
        down_weight, owned_down, first_down, second_down, bias_one, bias_two
    )
    return (
        result.reshape(tokens.shape),
        grad_tokens.reshape(tokens.shape),
        owned_norm1,
        owned_in,
        grad_conv,
        owned_out,
        owned_norm2,
        owned_gate_up,
        owned_down,
        new_norm1,
        new_in,
        new_conv,
        new_out,
        new_norm2,
        new_gate_up,
        new_down,
        new_first_norm1,
        new_first_in,
        new_first_conv,
        new_first_out,
        new_first_norm2,
        new_first_gate_up,
        new_first_down,
        new_second_norm1,
        new_second_in,
        new_second_conv,
        new_second_out,
        new_second_norm2,
        new_second_gate_up,
        new_second_down,
    )


def solution(mesh):
    n_dp, n_ctx, n_tp = (mesh.shape[name] for name in ("dp", "ctx", "tp"))
    n_lo = 2 if n_tp % 2 == 0 else 1
    devices = mesh.devices.reshape(n_dp, n_ctx, n_tp // n_lo, n_lo)
    paired = Mesh(devices, ("dp", "ctx", "hi", "lo"))
    tp = ("hi", "lo")

    row = P("dp", "ctx", None)
    params = (
        P(DATA),
        P(None, DATA, tp),
        P(None, tp),
        P(tp, DATA),
        P(DATA),
        P(None, DATA, tp),
        P(tp, DATA),
    )

    return jax.shard_map(
        per_device,
        mesh=paired,
        in_specs=(row, row, P("dp", None), *params, *params, *params),
        out_specs=(row, row, *params, *params, *params, *params),
        check_vma=False,
    )
```

```python
import functools

import jax
import jax.numpy as jnp
from jax import lax
from jax.experimental import pallas as pl
from jax.experimental.layout import Layout, with_layout_constraint
from jax.experimental.pallas import tpu as pltpu
from jax.sharding import Mesh, PartitionSpec as P


STEP = 5


EPS_NORM = 1e-05
BETA_ONE = 0.9
BETA_TWO = 0.95
LEARN_RATE = 0.01
DECAY_RATE = 0.1
ADAM_EPS = 1e-08

DATA = ("dp", "ctx")
MODEL = ("lo", "hi")


bf16 = jnp.bfloat16
f32 = jnp.float32


def doc_masks(lengths_row, count):
    positions = jnp.arange(count, dtype=jnp.int32)
    starts = jnp.cumsum(lengths_row) - lengths_row
    inside = starts[None, :] <= positions[:, None]
    doc_start = jnp.max(jnp.where(inside, starts[None, :], jnp.int32(0)), axis=1)
    mask_one = (positions - 1 >= doc_start).astype(f32)[:, None]
    mask_two = (positions - 2 >= doc_start).astype(f32)[:, None]
    return (mask_one, mask_two)


def rms_scale(inputs):
    return lax.rsqrt(jnp.mean(inputs * inputs, axis=-1, keepdims=True) + EPS_NORM)


def norm_back(grad_normed, unit_rows, gain_full, scale_rows):
    scaled = grad_normed * gain_full
    return scale_rows * (scaled - unit_rows * jnp.mean(scaled * unit_rows, axis=-1, keepdims=True))


def adamw(param, grads, first, second, bias_one, bias_two):
    new_first = BETA_ONE * first + (1.0 - BETA_ONE) * grads
    new_second = BETA_TWO * second + (1.0 - BETA_TWO) * grads * grads
    update = (
        new_first / bias_one / (jnp.sqrt(new_second / bias_two) + ADAM_EPS) + DECAY_RATE * param
    )
    return (param - LEARN_RATE * update, new_first, new_second)


def exchange(blocks, axes):
    return lax.all_to_all(blocks, axes, 0, 0, tiled=True)


def shift(block, k):
    n = lax.axis_size("dp")
    return lax.ppermute(block, "dp", [(i, (i + k) % n) for i in range(n)])


def fetch_all(block):
    return [block] + [shift(block, k) for k in range(1, lax.axis_size("dp"))]


def send_each(blocks):
    return [blocks[0]] + [shift(blocks[k], k) for k in range(1, lax.axis_size("dp"))]


def by_distance(blocks):
    n = lax.axis_size("dp")
    at = lax.axis_index("dp")
    return [lax.dynamic_index_in_dim(blocks, (at + k) % n, 0, keepdims=False) for k in range(n)]


def by_member(items):
    n = lax.axis_size("dp")
    at = lax.axis_index("dp")
    stacked = jnp.stack(items)
    return jnp.stack(
        [lax.dynamic_index_in_dim(stacked, (at - q) % n, 0, keepdims=False) for q in range(n)]
    )


def swap(block, axis):
    return lax.ppermute(block, axis, [(0, 1), (1, 0)])


def gather(block, axis):
    if lax.axis_size(axis) == 2:
        other = swap(block, axis)
        first = lax.axis_index(axis) == 0
        return jnp.stack([jnp.where(first, block, other), jnp.where(first, other, block)])
    return lax.all_gather(block, axis)


def sum_scatter(blocks, axis):
    if lax.axis_size(axis) == 2:
        mine = lax.axis_index(axis)
        kept = lax.dynamic_index_in_dim(blocks, mine, 0, keepdims=False)
        given = lax.dynamic_index_in_dim(blocks, 1 - mine, 0, keepdims=False)
        return kept.astype(f32) + swap(given, axis).astype(f32)
    return jnp.sum(exchange(blocks, axis).astype(f32), axis=0)


def gather_last(block, axis):
    if lax.axis_size(axis) == 2:
        other = swap(block, axis)
        first = lax.axis_index(axis) == 0
        return jnp.concatenate(
            [jnp.where(first, block, other), jnp.where(first, other, block)], axis=-1
        )
    return lax.all_gather(block, axis, axis=block.ndim - 1, tiled=True)


def gather_features(block):
    block = gather_last(block, "hi")
    return gather_last(block, "lo")


def row_major(block):
    return with_layout_constraint(block, Layout(major_to_minor=tuple(range(block.ndim))))


def dot_nt(left, right):
    return lax.dot_general(left, right, (((1,), (1,)), ((), ())), preferred_element_type=f32)


def dot_tn(left, right):
    return lax.dot_general(left, right, (((0,), (0,)), ((), ())), preferred_element_type=f32)


def ffn_body(n_dp, at, *refs):
    normed_own, normed_other, up_own, up_other = refs[:4]
    w_own = refs[4 : 4 + n_dp]
    w_other = refs[4 + n_dp : 4 + 2 * n_dp]
    kept_ffn, given_ffn, kept_grad, given_grad, kept_w, given_w = refs[4 + 2 * n_dp : 10 + 2 * n_dp]
    normed, upstream, weights, act, grad_gate, grad_up = refs[10 + 2 * n_dp :]
    f_three, lane = w_own[0].shape
    f_own = f_three // 3
    rows, half = normed_own.shape
    count = rows // n_dp
    n_hi = kept_ffn.shape[1]
    quarter = half // n_hi
    ctx_first = at[0] == 0
    lo_first = at[1] == 0

    def member(k):
        return lax.rem(at[2] + (n_dp - k), n_dp)

    def place(even, odd):
        for k in range(n_dp):
            left = pl.multiple_of(member(k) * (2 * lane), 2 * lane)
            weights[:, pl.ds(left, lane)] = even[k][...]
            weights[:, pl.ds(pl.multiple_of(left + lane, lane), lane)] = odd[k][...]

    @pl.when(ctx_first)
    def _():
        place(w_own, w_other)

    @pl.when(jnp.logical_not(ctx_first))
    def _():
        place(w_other, w_own)

    @pl.when(lo_first)
    def _():
        normed[:, :half] = normed_own[...]
        normed[:, half:] = normed_other[...]
        upstream[:, :half] = up_own[...]
        upstream[:, half:] = up_other[...]

    @pl.when(jnp.logical_not(lo_first))
    def _():
        normed[:, :half] = normed_other[...]
        normed[:, half:] = normed_own[...]
        upstream[:, :half] = up_other[...]
        upstream[:, half:] = up_own[...]

    tiles = 2
    tile = rows // tiles

    def step(i, carry):
        part = pl.ds(pl.multiple_of(i * tile, tile), tile)
        n_rows = normed[part, :]
        gate_pre = dot_nt(n_rows, weights[:f_own, :])
        up_pre = dot_nt(n_rows, weights[f_own : 2 * f_own, :])
        grad_act = dot_nt(upstream[part, :], weights[2 * f_own :, :])
        sig = 1.0 / (1.0 + jnp.exp(-gate_pre))
        gated = gate_pre * sig
        act[part, :] = (gated * up_pre).astype(bf16)
        grad_gate[part, :] = (grad_act * up_pre * sig * (1.0 + gate_pre * (1.0 - sig))).astype(bf16)
        grad_up[part, :] = (grad_act * gated).astype(bf16)

        def send(kept_out, given_out, values):
            kept = jnp.where(lo_first, values[:, :half], values[:, half:]).astype(bf16)
            given = jnp.where(lo_first, values[:, half:], values[:, :half]).astype(bf16)
            for j in range(n_dp // tiles):
                z = member(i * (n_dp // tiles) + j)
                for h in range(n_hi):
                    cut = (slice(j * count, (j + 1) * count), slice(h * quarter, (h + 1) * quarter))
                    kept_out[z, h] = kept[cut]
                    given_out[z, h] = given[cut]

        send(
            kept_ffn,
            given_ffn,
            jnp.dot(act[part, :], weights[2 * f_own :, :], preferred_element_type=f32),
        )
        send(
            kept_grad,
            given_grad,
            jnp.dot(grad_gate[part, :], weights[:f_own, :], preferred_element_type=f32)
            + jnp.dot(grad_up[part, :], weights[f_own : 2 * f_own, :], preferred_element_type=f32),
        )
        return carry

    lax.fori_loop(0, tiles, step, 0)

    for k, (left, right) in enumerate(((grad_gate, normed), (grad_up, normed), (act, upstream))):
        cut = slice(k * f_own, (k + 1) * f_own)
        for z in range(n_dp):
            away = lax.rem(z + n_dp - at[2], n_dp)
            pair = dot_tn(left[...], right[:, 2 * z * lane : (2 * z + 2) * lane])
            even = pair[:, :lane]
            odd = pair[:, lane:]
            kept_w[away, cut, :] = jnp.where(ctx_first, even, odd).astype(bf16)
            given_w[away, cut, :] = jnp.where(ctx_first, odd, even).astype(bf16)


def ffn_kernel(at, normed_own, normed_other, up_own, up_other, w_own, w_other, n_hi):
    n_dp = len(w_own)
    f_three, lane = w_own[0].shape
    rows, half = normed_own.shape
    parts = jax.ShapeDtypeStruct((n_dp, n_hi, rows // n_dp, half // n_hi), bf16)
    grads = jax.ShapeDtypeStruct((n_dp, f_three, lane), bf16)
    vmem = pl.BlockSpec(memory_space=pltpu.VMEM)
    hidden = pltpu.VMEM((rows, f_three // 3), bf16)
    return pl.pallas_call(
        functools.partial(ffn_body, n_dp),
        out_shape=(parts, parts, parts, parts, grads, grads),
        in_specs=[pl.BlockSpec(memory_space=pltpu.SMEM)] + [vmem] * (4 + 2 * n_dp),
        out_specs=[vmem] * 6,
        scratch_shapes=[
            pltpu.VMEM((rows, 2 * half), bf16),
            pltpu.VMEM((rows, 2 * half), bf16),
            pltpu.VMEM((f_three, 2 * n_dp * lane), bf16),
            hidden,
            hidden,
            hidden,
        ],
        compiler_params=pltpu.CompilerParams(vmem_limit_bytes=48 * 1024 * 1024),
        name="ffn",
    )(at, normed_own, normed_other, up_own, up_other, *w_own, *w_other)


def per_device(
    tokens,
    cotangent,
    doc_lengths,
    norm1_gain,
    in_weight,
    conv_weight,
    out_weight,
    norm2_gain,
    gate_up_weight,
    down_weight,
    first_norm1,
    first_in,
    first_conv,
    first_out,
    first_norm2,
    first_gate_up,
    first_down,
    second_norm1,
    second_in,
    second_conv,
    second_out,
    second_norm2,
    second_gate_up,
    second_down,
):
    n_dp = lax.axis_size("dp")
    n_ctx = lax.axis_size("ctx")
    n_hi = lax.axis_size("hi")
    n_lo = lax.axis_size("lo")
    n_tp = n_hi * n_lo
    n_data = n_dp * n_ctx
    at_ctx = lax.axis_index("ctx")
    at_lo = lax.axis_index("lo")

    rows = tokens.reshape(-1, tokens.shape[-1])
    upstream_f = cotangent.reshape(rows.shape)
    count, width = rows.shape
    length = count * n_ctx
    d_own = in_weight.shape[1]
    c_tp = in_weight.shape[2]
    c_own = c_tp // n_ctx
    f_tp = down_weight.shape[0]
    f_own = f_tp // n_dp
    half = width // n_lo
    quarter = width // n_tp

    mixer_own = jnp.concatenate([in_weight, out_weight.T[None]]).astype(bf16)
    mixer_own = mixer_own.reshape(4, d_own, n_ctx, c_own).transpose(2, 0, 1, 3)
    mixer_own = mixer_own.reshape(n_ctx, 4 * d_own, c_own)
    gains = jnp.concatenate([norm1_gain, norm2_gain]).astype(bf16)
    gains = jnp.pad(gains, (0, -gains.shape[0] % c_own)).reshape(-1, c_own)
    gains = jnp.broadcast_to(gains[None], (n_ctx, *gains.shape))
    mixer_own = jnp.concatenate([mixer_own, gains], axis=1)
    mixer_own = jnp.broadcast_to(mixer_own[None], (n_dp, *mixer_own.shape))
    mixer_all = exchange(mixer_own.reshape(n_data, -1, c_own), DATA)

    scale_one = rms_scale(rows)
    unit_one = rows * scale_one
    unit_seq = gather(unit_one.astype(bf16), "ctx").reshape(length, width)

    def half_rows(block):
        return lax.dynamic_slice_in_dim(block, at_lo * half, half, 1)

    ffn_own = jnp.concatenate(
        [gate_up_weight.astype(bf16).transpose(0, 2, 1), down_weight.astype(bf16)[None]]
    )
    ffn_own = ffn_own.reshape(3, n_dp, f_own, d_own).transpose(1, 0, 2, 3)
    ffn_own = by_distance(ffn_own.reshape(n_dp, 3 * f_own, d_own))
    own_other = swap(ffn_own[0], "ctx") if n_ctx == 2 else None
    at_quarter = at_lo * n_hi + lax.axis_index("hi")
    up_own = lax.dynamic_slice_in_dim(upstream_f.astype(bf16), at_quarter * quarter, quarter, 1)
    mixer_all, ffn_own, up_own = lax.optimization_barrier((mixer_all, ffn_own, up_own))
    ffn_own = send_each(ffn_own)
    up_own = jnp.concatenate(fetch_all(up_own))
    up_own = gather_last(up_own, "hi")

    w_mixer = mixer_all[:, : 4 * d_own].reshape(n_data, 4, d_own, c_own).transpose(1, 0, 2, 3)
    w_mixer = w_mixer.reshape(4, width, c_own)
    w_in = w_mixer[:3]
    w_out = w_mixer[3]
    gains_all = mixer_all[:, 4 * d_own :].reshape(n_data, -1).astype(f32)
    gain_one = gains_all[:, :d_own].reshape(width)
    gain_two = gains_all[:, d_own : 2 * d_own].reshape(width)
    normed_seq = (unit_seq.astype(f32) * gain_one).astype(bf16)

    mask_one, mask_two = doc_masks(doc_lengths[0], length + 2)
    taps = lax.dynamic_slice_in_dim(conv_weight, at_ctx * c_own, c_own, 1)
    projected = jnp.einsum("td,kdc->ktc", normed_seq, w_in, preferred_element_type=f32)
    gate_b = projected[0]
    gate_c = projected[1]
    values_x = projected[2]
    mixed_in = gate_b * values_x
    extended = jnp.pad(mixed_in, ((2, 0), (0, 0)))
    lag_one = extended[1 : length + 1] * mask_one[:length]
    lag_two = extended[:length] * mask_two[:length]
    conv_out = taps[0] * lag_two + taps[1] * lag_one + taps[2] * mixed_in
    gated_y = (gate_c * conv_out).astype(bf16)

    def mixer_sum(part):
        blocks = part.astype(bf16).reshape(n_ctx, count, n_tp, quarter).transpose(0, 2, 1, 3)
        blocks = exchange(blocks.reshape(n_ctx * n_tp, count, quarter), ("ctx", *MODEL))
        return jnp.sum(blocks.astype(f32), axis=0)

    mixer_part = dot_nt(gated_y, w_out)
    mixer_out = gather_features(mixer_sum(mixer_part).astype(bf16)).astype(f32)
    hidden_rows = rows + mixer_out
    scale_two = rms_scale(hidden_rows)
    unit_two = hidden_rows * scale_two
    normed_own = jnp.concatenate(fetch_all(half_rows((unit_two * gain_two).astype(bf16))))
    if n_ctx == 2 and n_lo == 2 and n_dp % 2 == 0 and d_own % 128 == 0 and f_own % 16 == 0:
        normed_other = swap(normed_own, "lo")
        up_other = swap(up_own, "lo")
        ffn_other = [own_other] + [swap(block, "ctx") for block in ffn_own[1:]]
        kept_ffn, given_ffn, kept_grad, given_grad, kept_w, given_w = ffn_kernel(
            jnp.stack([at_ctx, at_lo, lax.axis_index("dp")]),
            normed_own,
            normed_other,
            up_own,
            up_other,
            ffn_own,
            ffn_other,
            n_hi,
        )
        grad_part = (kept_grad.astype(f32) + swap(given_grad, "lo").astype(f32)).astype(bf16)
        ffn_part = (kept_ffn.astype(f32) + swap(given_ffn, "lo").astype(f32)).astype(bf16)
        grad_ffn = (kept_w.astype(f32) + swap(given_w, "ctx").astype(f32)).astype(bf16)
        grad_ffn = [grad_ffn[k] for k in range(n_dp)]
    else:
        by_order = by_member(list(normed_own.reshape(n_dp, count, half)))
        normed_two = gather_last(by_order.reshape(n_dp * count, half), "lo")
        by_order = by_member(list(up_own.reshape(n_dp, count, half)))
        upstream = gather_last(by_order.reshape(n_dp * count, half), "lo")
        w_ffn = gather(by_member(ffn_own), "ctx").reshape(n_ctx, n_dp, 3, f_own, d_own)
        w_ffn = w_ffn.transpose(2, 3, 1, 0, 4).reshape(3, f_own, width)
        w_gate_up = w_ffn[:2]
        w_down = w_ffn[2]
        gate_up = jnp.einsum("td,kfd->ktf", normed_two, w_gate_up, preferred_element_type=f32)
        gate_pre = gate_up[0]
        up_pre = gate_up[1]
        sig = jax.nn.sigmoid(gate_pre)
        activated = (gate_pre * sig * up_pre).astype(bf16)
        grad_act = dot_nt(upstream, w_down)
        grad_gate = (grad_act * up_pre * sig * (1.0 + gate_pre * (1.0 - sig))).astype(bf16)
        grad_up = (grad_act * gate_pre * sig).astype(bf16)
        both = jnp.stack([grad_gate, grad_up])

        def sum_pairs(part):
            part = part.astype(bf16).reshape(n_dp * count, n_lo, half).transpose(1, 0, 2)
            part = sum_scatter(part, "lo").astype(bf16)
            return part.reshape(n_dp, count, n_hi, quarter).transpose(0, 2, 1, 3)

        ffn_part = sum_pairs(jnp.dot(activated, w_down, preferred_element_type=f32))
        grad_part = sum_pairs(
            jnp.einsum("ktf,kfd->td", both, w_gate_up, preferred_element_type=f32)
        )
        grad_gate_up = jnp.einsum("ktf,td->kfd", both, normed_two, preferred_element_type=f32)
        grad_down = dot_tn(activated, upstream)
        grad_ffn = jnp.concatenate([grad_gate_up.astype(bf16), grad_down.astype(bf16)[None]])
        grad_ffn = grad_ffn.reshape(3 * f_own, n_dp, n_ctx, d_own).transpose(2, 1, 0, 3)
        grad_ffn = by_distance(sum_scatter(grad_ffn, "ctx").astype(bf16))

    grad_part = exchange(grad_part.reshape(n_dp * n_hi, count, quarter), ("dp", "hi"))
    grad_part, ffn_part, grad_ffn = lax.optimization_barrier((grad_part, ffn_part, grad_ffn))
    grad_ffn = send_each(grad_ffn)
    grad_part = jnp.sum(grad_part.astype(f32), axis=0).astype(bf16)
    grad_normed_two = gather_features(grad_part).astype(f32)

    ffn_part = sum_scatter(ffn_part.transpose(1, 0, 2, 3), "hi").astype(bf16)
    ffn_part = by_distance(ffn_part)
    ffn_part = send_each(ffn_part)

    grad_norm2 = jnp.sum(grad_normed_two * unit_two, axis=0)
    grad_hidden = upstream_f + norm_back(grad_normed_two, unit_two, gain_two, scale_two)
    grad_seq = gather(grad_hidden.astype(bf16), "ctx").reshape(length, width)

    grad_y = jnp.dot(grad_seq, w_out, preferred_element_type=f32)
    grad_out = dot_tn(grad_seq, gated_y)
    grad_c = grad_y * conv_out
    grad_conv_in = grad_y * gate_c
    grad_ext = jnp.pad(grad_conv_in, ((0, 2), (0, 0)))
    lead_one = (grad_ext * mask_one)[1 : length + 1]
    lead_two = (grad_ext * mask_two)[2:]
    grad_mixed = taps[2] * grad_conv_in + taps[1] * lead_one + taps[0] * lead_two
    grad_taps = jnp.stack(
        [
            jnp.sum(grad_conv_in * lag_two, axis=0),
            jnp.sum(grad_conv_in * lag_one, axis=0),
            jnp.sum(grad_conv_in * mixed_in, axis=0),
        ]
    )
    grad_gates = jnp.stack(
        [
            (grad_mixed * values_x).astype(bf16),
            grad_c.astype(bf16),
            (grad_mixed * gate_b).astype(bf16),
        ]
    )
    ffn_part, grad_ffn, _ = lax.optimization_barrier((ffn_part, grad_ffn, grad_gates))
    ffn_part = functools.reduce(jnp.add, [part.astype(f32) for part in ffn_part]).astype(bf16)
    result = hidden_rows + gather_features(ffn_part).astype(f32)
    grad_ffn = by_member(grad_ffn).reshape(n_dp, 3, f_own, d_own).transpose(1, 0, 2, 3)
    grad_ffn = grad_ffn.reshape(3, f_tp, d_own)
    owned_gate_up = row_major(grad_ffn[:2].transpose(0, 2, 1)).astype(f32)
    owned_down = grad_ffn[2].astype(f32)

    grad_in = jnp.einsum("td,ktc->kdc", normed_seq, grad_gates, preferred_element_type=f32)
    grad_mixer = jnp.concatenate([grad_in.astype(bf16), grad_out.astype(bf16)[None]])
    grad_mixer = grad_mixer.reshape(4, n_dp, n_ctx, d_own, c_own).transpose(1, 2, 0, 3, 4)
    grad_mixer = by_distance(grad_mixer.reshape(n_dp, n_ctx, 4 * d_own, c_own))
    grad_mixer = send_each(grad_mixer)
    grad_mixer = functools.reduce(jnp.add, [block.astype(f32) for block in grad_mixer])
    if n_ctx == 2:
        kept = lax.dynamic_index_in_dim(grad_mixer, at_ctx, 0, keepdims=False)
        given = lax.dynamic_index_in_dim(grad_mixer, 1 - at_ctx, 0, keepdims=False)
        other = swap(given.astype(bf16), "ctx").astype(f32)
        first = at_ctx == 0
        owned_mixer = jnp.stack([jnp.where(first, kept, other), jnp.where(first, other, kept)])
    else:
        owned_mixer = exchange(grad_mixer.astype(bf16), "ctx").astype(f32)
    owned_mixer = owned_mixer.reshape(n_ctx, 4, d_own, c_own).transpose(1, 2, 0, 3)
    owned_mixer = owned_mixer.reshape(4, d_own, c_tp)
    owned_in = row_major(owned_mixer[:3])
    owned_out = row_major(owned_mixer[3].T)

    normed_one_part = jnp.einsum("ktc,kdc->td", grad_gates, w_in, preferred_element_type=f32)
    grad_normed_one = gather_features(mixer_sum(normed_one_part).astype(bf16))
    grad_normed_one = grad_normed_one.astype(f32)
    grad_norm1 = jnp.sum(grad_normed_one * unit_one, axis=0)
    grad_tokens = grad_hidden + norm_back(grad_normed_one, unit_one, gain_one, scale_one)

    small = jnp.concatenate(
        [
            grad_norm1.reshape(n_data, d_own),
            grad_norm2.reshape(n_data, d_own),
            jnp.broadcast_to(grad_taps.reshape(1, -1), (n_data, grad_taps.size)),
        ],
        axis=1,
    )
    small = exchange(small, DATA)
    small = jnp.sum(small.reshape(n_dp, n_ctx, -1), axis=0)
    owned_norm1 = jnp.sum(small[:, :d_own], axis=0)
    owned_norm2 = jnp.sum(small[:, d_own : 2 * d_own], axis=0)
    grad_conv = small[:, 2 * d_own :].reshape(n_ctx, 3, c_own)
    grad_conv = grad_conv.transpose(1, 0, 2).reshape(3, c_tp)

    steps = jnp.float32(STEP)
    bias_one = 1.0 - jnp.power(jnp.float32(BETA_ONE), steps)
    bias_two = 1.0 - jnp.power(jnp.float32(BETA_TWO), steps)
    new_norm1, new_first_norm1, new_second_norm1 = adamw(
        norm1_gain, owned_norm1, first_norm1, second_norm1, bias_one, bias_two
    )
    new_in, new_first_in, new_second_in = adamw(
        in_weight, owned_in, first_in, second_in, bias_one, bias_two
    )
    new_conv, new_first_conv, new_second_conv = adamw(
        conv_weight, grad_conv, first_conv, second_conv, bias_one, bias_two
    )
    new_out, new_first_out, new_second_out = adamw(
        out_weight, owned_out, first_out, second_out, bias_one, bias_two
    )
    new_norm2, new_first_norm2, new_second_norm2 = adamw(
        norm2_gain, owned_norm2, first_norm2, second_norm2, bias_one, bias_two
    )
    new_gate_up, new_first_gate_up, new_second_gate_up = adamw(
        gate_up_weight, owned_gate_up, first_gate_up, second_gate_up, bias_one, bias_two
    )
    new_down, new_first_down, new_second_down = adamw(
        down_weight, owned_down, first_down, second_down, bias_one, bias_two
    )
    return (
        result.reshape(tokens.shape),
        grad_tokens.reshape(tokens.shape),
        owned_norm1,
        owned_in,
        grad_conv,
        owned_out,
        owned_norm2,
        owned_gate_up,
        owned_down,
        new_norm1,
        new_in,
        new_conv,
        new_out,
        new_norm2,
        new_gate_up,
        new_down,
        new_first_norm1,
        new_first_in,
        new_first_conv,
        new_first_out,
        new_first_norm2,
        new_first_gate_up,
        new_first_down,
        new_second_norm1,
        new_second_in,
        new_second_conv,
        new_second_out,
        new_second_norm2,
        new_second_gate_up,
        new_second_down,
    )


def solution(mesh):
    n_dp, n_ctx, n_tp = (mesh.shape[name] for name in ("dp", "ctx", "tp"))
    n_lo = 2 if n_tp % 2 == 0 else 1
    devices = mesh.devices.reshape(n_dp, n_ctx, n_tp // n_lo, n_lo)
    paired = Mesh(devices, ("dp", "ctx", "hi", "lo"))
    tp = ("hi", "lo")

    row = P("dp", "ctx", None)
    params = (
        P(DATA),
        P(None, DATA, tp),
        P(None, tp),
        P(tp, DATA),
        P(DATA),
        P(None, DATA, tp),
        P(tp, DATA),
    )

    return jax.shard_map(
        per_device,
        mesh=paired,
        in_specs=(row, row, P("dp", None), *params, *params, *params),
        out_specs=(row, row, *params, *params, *params, *params),
        check_vma=False,
    )
```

```python
import functools

import jax
import jax.numpy as jnp
from jax import lax
from jax.experimental import pallas as pl
from jax.experimental.layout import Layout, with_layout_constraint
from jax.experimental.pallas import tpu as pltpu
from jax.sharding import Mesh, PartitionSpec as P


STEP = 5


EPS_NORM = 1e-05
BETA_ONE = 0.9
BETA_TWO = 0.95
LEARN_RATE = 0.01
DECAY_RATE = 0.1
ADAM_EPS = 1e-08

DATA = ("dp", "ctx")
MODEL = ("lo", "hi")


bf16 = jnp.bfloat16
f32 = jnp.float32


def doc_masks(lengths_row, count):
    positions = jnp.arange(count, dtype=jnp.int32)
    starts = jnp.cumsum(lengths_row) - lengths_row
    inside = starts[None, :] <= positions[:, None]
    doc_start = jnp.max(jnp.where(inside, starts[None, :], jnp.int32(0)), axis=1)
    mask_one = (positions - 1 >= doc_start).astype(f32)[:, None]
    mask_two = (positions - 2 >= doc_start).astype(f32)[:, None]
    return (mask_one, mask_two)


def rms_scale(inputs):
    return lax.rsqrt(jnp.mean(inputs * inputs, axis=-1, keepdims=True) + EPS_NORM)


def norm_back(grad_normed, unit_rows, gain_full, scale_rows):
    scaled = grad_normed * gain_full
    return scale_rows * (scaled - unit_rows * jnp.mean(scaled * unit_rows, axis=-1, keepdims=True))


def adamw(param, grads, first, second, bias_one, bias_two):
    new_first = BETA_ONE * first + (1.0 - BETA_ONE) * grads
    new_second = BETA_TWO * second + (1.0 - BETA_TWO) * grads * grads
    update = (
        new_first / bias_one / (jnp.sqrt(new_second / bias_two) + ADAM_EPS) + DECAY_RATE * param
    )
    return (param - LEARN_RATE * update, new_first, new_second)


def exchange(blocks, axes):
    return lax.all_to_all(blocks, axes, 0, 0, tiled=True)


def shift(block, k):
    n = lax.axis_size("dp")
    return lax.ppermute(block, "dp", [(i, (i + k) % n) for i in range(n)])


def fetch_all(block):
    return [block] + [shift(block, k) for k in range(1, lax.axis_size("dp"))]


def send_each(blocks):
    return [blocks[0]] + [shift(blocks[k], k) for k in range(1, lax.axis_size("dp"))]


def by_distance(blocks):
    n = lax.axis_size("dp")
    at = lax.axis_index("dp")
    return [lax.dynamic_index_in_dim(blocks, (at + k) % n, 0, keepdims=False) for k in range(n)]


def by_member(items):
    n = lax.axis_size("dp")
    at = lax.axis_index("dp")
    stacked = jnp.stack(items)
    return jnp.stack(
        [lax.dynamic_index_in_dim(stacked, (at - q) % n, 0, keepdims=False) for q in range(n)]
    )


def swap(block, axis):
    return lax.ppermute(block, axis, [(0, 1), (1, 0)])


def gather(block, axis):
    if lax.axis_size(axis) == 2:
        other = swap(block, axis)
        first = lax.axis_index(axis) == 0
        return jnp.stack([jnp.where(first, block, other), jnp.where(first, other, block)])
    return lax.all_gather(block, axis)


def sum_scatter(blocks, axis):
    if lax.axis_size(axis) == 2:
        mine = lax.axis_index(axis)
        kept = lax.dynamic_index_in_dim(blocks, mine, 0, keepdims=False)
        given = lax.dynamic_index_in_dim(blocks, 1 - mine, 0, keepdims=False)
        given = swap(given, axis)
        return kept.astype(f32) + given.astype(f32)
    return jnp.sum(exchange(blocks, axis).astype(f32), axis=0)


def gather_last(block, axis):
    if lax.axis_size(axis) == 2:
        other = swap(block, axis)
        first = lax.axis_index(axis) == 0
        return jnp.concatenate(
            [jnp.where(first, block, other), jnp.where(first, other, block)], axis=-1
        )
    return lax.all_gather(block, axis, axis=block.ndim - 1, tiled=True)


def gather_features(block):
    block = gather_last(block, "hi")
    return gather_last(block, "lo")


def row_major(block):
    return with_layout_constraint(block, Layout(major_to_minor=tuple(range(block.ndim))))


def dot_nt(left, right):
    return lax.dot_general(left, right, (((1,), (1,)), ((), ())), preferred_element_type=f32)


def dot_tn(left, right):
    return lax.dot_general(left, right, (((0,), (0,)), ((), ())), preferred_element_type=f32)


def ffn_body(n_dp, at, *refs):
    normed_own, normed_other, up_own, up_other = refs[:4]
    w_own = refs[4 : 4 + n_dp]
    w_other = refs[4 + n_dp : 4 + 2 * n_dp]
    kept_ffn, given_ffn, kept_grad, given_grad, kept_w, given_w = refs[4 + 2 * n_dp : 10 + 2 * n_dp]
    normed, upstream, weights, act, grad_gate, grad_up = refs[10 + 2 * n_dp :]
    f_three, lane = w_own[0].shape
    f_own = f_three // 3
    rows, half = normed_own.shape
    count = rows // n_dp
    n_hi = kept_ffn.shape[1]
    quarter = half // n_hi
    ctx_first = at[0] == 0
    lo_first = at[1] == 0

    def member(k):
        return lax.rem(at[2] + (n_dp - k), n_dp)

    def place(even, odd):
        for k in range(n_dp):
            left = pl.multiple_of(member(k) * (2 * lane), 2 * lane)
            weights[:, pl.ds(left, lane)] = even[k][...]
            weights[:, pl.ds(pl.multiple_of(left + lane, lane), lane)] = odd[k][...]

    @pl.when(ctx_first)
    def _():
        place(w_own, w_other)

    @pl.when(jnp.logical_not(ctx_first))
    def _():
        place(w_other, w_own)

    @pl.when(lo_first)
    def _():
        normed[:, :half] = normed_own[...]
        normed[:, half:] = normed_other[...]
        upstream[:, :half] = up_own[...]
        upstream[:, half:] = up_other[...]

    @pl.when(jnp.logical_not(lo_first))
    def _():
        normed[:, :half] = normed_other[...]
        normed[:, half:] = normed_own[...]
        upstream[:, :half] = up_other[...]
        upstream[:, half:] = up_own[...]

    tiles = 2
    tile = rows // tiles

    def step(i, carry):
        part = pl.ds(pl.multiple_of(i * tile, tile), tile)
        n_rows = normed[part, :]
        gate_pre = dot_nt(n_rows, weights[:f_own, :])
        up_pre = dot_nt(n_rows, weights[f_own : 2 * f_own, :])
        grad_act = dot_nt(upstream[part, :], weights[2 * f_own :, :])
        sig = 1.0 / (1.0 + jnp.exp(-gate_pre))
        gated = gate_pre * sig
        act[part, :] = (gated * up_pre).astype(bf16)
        grad_gate[part, :] = (grad_act * up_pre * sig * (1.0 + gate_pre * (1.0 - sig))).astype(bf16)
        grad_up[part, :] = (grad_act * gated).astype(bf16)

        def send(kept_out, given_out, values):
            kept = jnp.where(lo_first, values[:, :half], values[:, half:]).astype(bf16)
            given = jnp.where(lo_first, values[:, half:], values[:, :half]).astype(bf16)
            for j in range(n_dp // tiles):
                z = member(i * (n_dp // tiles) + j)
                for h in range(n_hi):
                    cut = (slice(j * count, (j + 1) * count), slice(h * quarter, (h + 1) * quarter))
                    kept_out[z, h] = kept[cut]
                    given_out[z, h] = given[cut]

        send(
            kept_ffn,
            given_ffn,
            jnp.dot(act[part, :], weights[2 * f_own :, :], preferred_element_type=f32),
        )
        send(
            kept_grad,
            given_grad,
            jnp.dot(grad_gate[part, :], weights[:f_own, :], preferred_element_type=f32)
            + jnp.dot(grad_up[part, :], weights[f_own : 2 * f_own, :], preferred_element_type=f32),
        )
        return carry

    lax.fori_loop(0, tiles, step, 0)

    for k, (left, right) in enumerate(((grad_gate, normed), (grad_up, normed), (act, upstream))):
        cut = slice(k * f_own, (k + 1) * f_own)
        for z in range(n_dp):
            away = lax.rem(z + n_dp - at[2], n_dp)
            pair = dot_tn(left[...], right[:, 2 * z * lane : (2 * z + 2) * lane])
            even = pair[:, :lane]
            odd = pair[:, lane:]
            kept_w[away, cut, :] = jnp.where(ctx_first, even, odd).astype(bf16)
            given_w[away, cut, :] = jnp.where(ctx_first, odd, even).astype(bf16)


def ffn_kernel(at, normed_own, normed_other, up_own, up_other, w_own, w_other, n_hi):
    n_dp = len(w_own)
    f_three, lane = w_own[0].shape
    rows, half = normed_own.shape
    parts = jax.ShapeDtypeStruct((n_dp, n_hi, rows // n_dp, half // n_hi), bf16)
    grads = jax.ShapeDtypeStruct((n_dp, f_three, lane), bf16)
    vmem = pl.BlockSpec(memory_space=pltpu.VMEM)
    hidden = pltpu.VMEM((rows, f_three // 3), bf16)
    return pl.pallas_call(
        functools.partial(ffn_body, n_dp),
        out_shape=(parts, parts, parts, parts, grads, grads),
        in_specs=[pl.BlockSpec(memory_space=pltpu.SMEM)] + [vmem] * (4 + 2 * n_dp),
        out_specs=[vmem] * 6,
        scratch_shapes=[
            pltpu.VMEM((rows, 2 * half), bf16),
            pltpu.VMEM((rows, 2 * half), bf16),
            pltpu.VMEM((f_three, 2 * n_dp * lane), bf16),
            hidden,
            hidden,
            hidden,
        ],
        compiler_params=pltpu.CompilerParams(vmem_limit_bytes=48 * 1024 * 1024),
        name="ffn",
    )(at, normed_own, normed_other, up_own, up_other, *w_own, *w_other)


def per_device(
    tokens,
    cotangent,
    doc_lengths,
    norm1_gain,
    in_weight,
    conv_weight,
    out_weight,
    norm2_gain,
    gate_up_weight,
    down_weight,
    first_norm1,
    first_in,
    first_conv,
    first_out,
    first_norm2,
    first_gate_up,
    first_down,
    second_norm1,
    second_in,
    second_conv,
    second_out,
    second_norm2,
    second_gate_up,
    second_down,
):
    n_dp = lax.axis_size("dp")
    n_ctx = lax.axis_size("ctx")
    n_hi = lax.axis_size("hi")
    n_lo = lax.axis_size("lo")
    n_tp = n_hi * n_lo
    n_data = n_dp * n_ctx
    at_ctx = lax.axis_index("ctx")
    at_lo = lax.axis_index("lo")

    rows = tokens.reshape(-1, tokens.shape[-1])
    upstream_f = cotangent.reshape(rows.shape)
    count, width = rows.shape
    length = count * n_ctx
    d_own = in_weight.shape[1]
    c_tp = in_weight.shape[2]
    c_own = c_tp // n_ctx
    f_tp = down_weight.shape[0]
    f_own = f_tp // n_dp
    half = width // n_lo
    quarter = width // n_tp

    mixer_own = jnp.concatenate([in_weight, out_weight.T[None]]).astype(bf16)
    mixer_own = mixer_own.reshape(4, d_own, n_ctx, c_own).transpose(2, 0, 1, 3)
    mixer_own = mixer_own.reshape(n_ctx, 4 * d_own, c_own)
    gains = jnp.concatenate([norm1_gain, norm2_gain]).astype(bf16)
    gains = jnp.pad(gains, (0, -gains.shape[0] % c_own)).reshape(-1, c_own)
    gains = jnp.broadcast_to(gains[None], (n_ctx, *gains.shape))
    mixer_own = jnp.concatenate([mixer_own, gains], axis=1)
    mixer_own = jnp.broadcast_to(mixer_own[None], (n_dp, *mixer_own.shape))
    mixer_all = exchange(mixer_own.reshape(n_data, -1, c_own), DATA)

    scale_one = rms_scale(rows)
    unit_one = rows * scale_one
    unit_seq = gather(unit_one.astype(bf16), "ctx").reshape(length, width)

    def half_rows(block):
        return lax.dynamic_slice_in_dim(block, at_lo * half, half, 1)

    ffn_own = jnp.concatenate(
        [gate_up_weight.astype(bf16).transpose(0, 2, 1), down_weight.astype(bf16)[None]]
    )
    ffn_own = ffn_own.reshape(3, n_dp, f_own, d_own).transpose(1, 0, 2, 3)
    ffn_own = by_distance(ffn_own.reshape(n_dp, 3 * f_own, d_own))
    own_other = swap(ffn_own[0], "ctx") if n_ctx == 2 else None
    at_quarter = at_lo * n_hi + lax.axis_index("hi")
    up_own = lax.dynamic_slice_in_dim(upstream_f.astype(bf16), at_quarter * quarter, quarter, 1)
    mixer_all, ffn_own, up_own = lax.optimization_barrier((mixer_all, ffn_own, up_own))
    ffn_own = send_each(ffn_own)
    up_own = jnp.concatenate(fetch_all(up_own))
    up_own = gather_last(up_own, "hi")

    w_mixer = mixer_all[:, : 4 * d_own].reshape(n_data, 4, d_own, c_own).transpose(1, 0, 2, 3)
    w_mixer = w_mixer.reshape(4, width, c_own)
    w_in = w_mixer[:3]
    w_out = w_mixer[3]
    gains_all = mixer_all[:, 4 * d_own :].reshape(n_data, -1).astype(f32)
    gain_one = gains_all[:, :d_own].reshape(width)
    gain_two = gains_all[:, d_own : 2 * d_own].reshape(width)
    normed_seq = (unit_seq.astype(f32) * gain_one).astype(bf16)

    mask_one, mask_two = doc_masks(doc_lengths[0], length + 2)
    taps = lax.dynamic_slice_in_dim(conv_weight, at_ctx * c_own, c_own, 1)
    projected = jnp.einsum("td,kdc->ktc", normed_seq, w_in, preferred_element_type=f32)
    gate_b = projected[0]
    gate_c = projected[1]
    values_x = projected[2]
    mixed_in = gate_b * values_x
    extended = jnp.pad(mixed_in, ((2, 0), (0, 0)))
    lag_one = extended[1 : length + 1] * mask_one[:length]
    lag_two = extended[:length] * mask_two[:length]
    conv_out = taps[0] * lag_two + taps[1] * lag_one + taps[2] * mixed_in
    gated_y = (gate_c * conv_out).astype(bf16)

    def mixer_sum(part):
        blocks = part.astype(bf16).reshape(n_ctx, count, n_tp, quarter).transpose(0, 2, 1, 3)
        blocks = exchange(blocks.reshape(n_ctx * n_tp, count, quarter), ("ctx", *MODEL))
        return jnp.sum(blocks.astype(f32), axis=0)

    mixer_part = dot_nt(gated_y, w_out)
    mixer_out = gather_features(mixer_sum(mixer_part).astype(bf16)).astype(f32)
    hidden_rows = rows + mixer_out
    scale_two = rms_scale(hidden_rows)
    unit_two = hidden_rows * scale_two
    normed_own = jnp.concatenate(fetch_all(half_rows((unit_two * gain_two).astype(bf16))))
    if n_ctx == 2 and n_lo == 2 and n_dp % 2 == 0 and d_own % 128 == 0 and f_own % 16 == 0:
        normed_other = swap(normed_own, "lo")
        up_other = swap(up_own, "lo")
        ffn_other = [own_other] + [swap(block, "ctx") for block in ffn_own[1:]]
        kept_ffn, given_ffn, kept_grad, given_grad, kept_w, given_w = ffn_kernel(
            jnp.stack([at_ctx, at_lo, lax.axis_index("dp")]),
            normed_own,
            normed_other,
            up_own,
            up_other,
            ffn_own,
            ffn_other,
            n_hi,
        )
        grad_part = (kept_grad.astype(f32) + swap(given_grad, "lo").astype(f32)).astype(bf16)
        ffn_part = (kept_ffn.astype(f32) + swap(given_ffn, "lo").astype(f32)).astype(bf16)
        grad_ffn = (kept_w.astype(f32) + swap(given_w, "ctx").astype(f32)).astype(bf16)
        grad_ffn = [grad_ffn[k] for k in range(n_dp)]
    else:
        by_order = by_member(list(normed_own.reshape(n_dp, count, half)))
        normed_two = gather_last(by_order.reshape(n_dp * count, half), "lo")
        by_order = by_member(list(up_own.reshape(n_dp, count, half)))
        upstream = gather_last(by_order.reshape(n_dp * count, half), "lo")
        w_ffn = gather(by_member(ffn_own), "ctx").reshape(n_ctx, n_dp, 3, f_own, d_own)
        w_ffn = w_ffn.transpose(2, 3, 1, 0, 4).reshape(3, f_own, width)
        w_gate_up = w_ffn[:2]
        w_down = w_ffn[2]
        gate_up = jnp.einsum("td,kfd->ktf", normed_two, w_gate_up, preferred_element_type=f32)
        gate_pre = gate_up[0]
        up_pre = gate_up[1]
        sig = jax.nn.sigmoid(gate_pre)
        activated = (gate_pre * sig * up_pre).astype(bf16)
        grad_act = dot_nt(upstream, w_down)
        grad_gate = (grad_act * up_pre * sig * (1.0 + gate_pre * (1.0 - sig))).astype(bf16)
        grad_up = (grad_act * gate_pre * sig).astype(bf16)
        both = jnp.stack([grad_gate, grad_up])

        def sum_pairs(part):
            part = part.astype(bf16).reshape(n_dp * count, n_lo, half).transpose(1, 0, 2)
            part = sum_scatter(part, "lo").astype(bf16)
            return part.reshape(n_dp, count, n_hi, quarter).transpose(0, 2, 1, 3)

        ffn_part = sum_pairs(jnp.dot(activated, w_down, preferred_element_type=f32))
        grad_part = sum_pairs(
            jnp.einsum("ktf,kfd->td", both, w_gate_up, preferred_element_type=f32)
        )
        grad_gate_up = jnp.einsum("ktf,td->kfd", both, normed_two, preferred_element_type=f32)
        grad_down = dot_tn(activated, upstream)
        grad_ffn = jnp.concatenate([grad_gate_up.astype(bf16), grad_down.astype(bf16)[None]])
        grad_ffn = grad_ffn.reshape(3 * f_own, n_dp, n_ctx, d_own).transpose(2, 1, 0, 3)
        grad_ffn = by_distance(sum_scatter(grad_ffn, "ctx").astype(bf16))

    grad_part = exchange(grad_part.reshape(n_dp * n_hi, count, quarter), ("dp", "hi"))
    grad_ffn = send_each(grad_ffn)
    grad_part = jnp.sum(grad_part.astype(f32), axis=0).astype(bf16)
    grad_normed_two = gather_features(grad_part).astype(f32)

    ffn_part = sum_scatter(ffn_part.transpose(1, 0, 2, 3), "hi").astype(bf16)
    ffn_part = by_distance(ffn_part)
    ffn_part = send_each(ffn_part)

    grad_norm2 = jnp.sum(grad_normed_two * unit_two, axis=0)
    grad_hidden = upstream_f + norm_back(grad_normed_two, unit_two, gain_two, scale_two)
    grad_seq = gather(grad_hidden.astype(bf16), "ctx").reshape(length, width)

    grad_y = jnp.dot(grad_seq, w_out, preferred_element_type=f32)
    grad_out = dot_tn(grad_seq, gated_y)
    grad_c = grad_y * conv_out
    grad_conv_in = grad_y * gate_c
    grad_ext = jnp.pad(grad_conv_in, ((0, 2), (0, 0)))
    lead_one = (grad_ext * mask_one)[1 : length + 1]
    lead_two = (grad_ext * mask_two)[2:]
    grad_mixed = taps[2] * grad_conv_in + taps[1] * lead_one + taps[0] * lead_two
    grad_taps = jnp.stack(
        [
            jnp.sum(grad_conv_in * lag_two, axis=0),
            jnp.sum(grad_conv_in * lag_one, axis=0),
            jnp.sum(grad_conv_in * mixed_in, axis=0),
        ]
    )
    grad_gates = jnp.stack(
        [
            (grad_mixed * values_x).astype(bf16),
            grad_c.astype(bf16),
            (grad_mixed * gate_b).astype(bf16),
        ]
    )
    grad_ffn = by_member(grad_ffn).reshape(n_dp, 3, f_own, d_own).transpose(1, 0, 2, 3)
    grad_ffn = grad_ffn.reshape(3, f_tp, d_own)
    owned_gate_up = row_major(grad_ffn[:2].transpose(0, 2, 1)).astype(f32)
    owned_down = grad_ffn[2].astype(f32)
    steps = jnp.float32(STEP)
    bias_one = 1.0 - jnp.power(jnp.float32(BETA_ONE), steps)
    bias_two = 1.0 - jnp.power(jnp.float32(BETA_TWO), steps)
    new_gate_up, new_first_gate_up, new_second_gate_up = adamw(
        gate_up_weight, owned_gate_up, first_gate_up, second_gate_up, bias_one, bias_two
    )
    new_down, new_first_down, new_second_down = adamw(
        down_weight, owned_down, first_down, second_down, bias_one, bias_two
    )
    ffn_part = functools.reduce(jnp.add, [part.astype(f32) for part in ffn_part]).astype(bf16)
    result = hidden_rows + gather_features(ffn_part).astype(f32)

    grad_in = jnp.einsum("td,ktc->kdc", normed_seq, grad_gates, preferred_element_type=f32)
    grad_mixer = jnp.concatenate([grad_in.astype(bf16), grad_out.astype(bf16)[None]])
    grad_mixer = grad_mixer.reshape(4, n_dp, n_ctx, d_own, c_own).transpose(1, 2, 0, 3, 4)
    grad_mixer = by_distance(grad_mixer.reshape(n_dp, n_ctx, 4 * d_own, c_own))
    grad_mixer = send_each(grad_mixer)
    grad_mixer = functools.reduce(jnp.add, [block.astype(f32) for block in grad_mixer])
    if n_ctx == 2:
        kept = lax.dynamic_index_in_dim(grad_mixer, at_ctx, 0, keepdims=False)
        given = lax.dynamic_index_in_dim(grad_mixer, 1 - at_ctx, 0, keepdims=False)
        other = swap(given.astype(bf16), "ctx").astype(f32)
        first = at_ctx == 0
        owned_mixer = jnp.stack([jnp.where(first, kept, other), jnp.where(first, other, kept)])
    else:
        owned_mixer = exchange(grad_mixer.astype(bf16), "ctx").astype(f32)
    owned_mixer = owned_mixer.reshape(n_ctx, 4, d_own, c_own).transpose(1, 2, 0, 3)
    owned_mixer = owned_mixer.reshape(4, d_own, c_tp)
    owned_in = row_major(owned_mixer[:3])
    owned_out = row_major(owned_mixer[3].T)

    normed_one_part = jnp.einsum("ktc,kdc->td", grad_gates, w_in, preferred_element_type=f32)
    grad_normed_one = gather_features(mixer_sum(normed_one_part).astype(bf16))
    grad_normed_one = grad_normed_one.astype(f32)
    grad_norm1 = jnp.sum(grad_normed_one * unit_one, axis=0)
    grad_tokens = grad_hidden + norm_back(grad_normed_one, unit_one, gain_one, scale_one)

    small = jnp.concatenate(
        [
            grad_norm1.reshape(n_data, d_own),
            grad_norm2.reshape(n_data, d_own),
            jnp.broadcast_to(grad_taps.reshape(1, -1), (n_data, grad_taps.size)),
        ],
        axis=1,
    )
    small = exchange(small, DATA)
    small = jnp.sum(small.reshape(n_dp, n_ctx, -1), axis=0)
    owned_norm1 = jnp.sum(small[:, :d_own], axis=0)
    owned_norm2 = jnp.sum(small[:, d_own : 2 * d_own], axis=0)
    grad_conv = small[:, 2 * d_own :].reshape(n_ctx, 3, c_own)
    grad_conv = grad_conv.transpose(1, 0, 2).reshape(3, c_tp)

    new_norm1, new_first_norm1, new_second_norm1 = adamw(
        norm1_gain, owned_norm1, first_norm1, second_norm1, bias_one, bias_two
    )
    new_in, new_first_in, new_second_in = adamw(
        in_weight, owned_in, first_in, second_in, bias_one, bias_two
    )
    new_out, new_first_out, new_second_out = adamw(
        out_weight, owned_out, first_out, second_out, bias_one, bias_two
    )
    new_conv, new_first_conv, new_second_conv = adamw(
        conv_weight, grad_conv, first_conv, second_conv, bias_one, bias_two
    )
    new_norm2, new_first_norm2, new_second_norm2 = adamw(
        norm2_gain, owned_norm2, first_norm2, second_norm2, bias_one, bias_two
    )
    return (
        result.reshape(tokens.shape),
        grad_tokens.reshape(tokens.shape),
        owned_norm1,
        owned_in,
        grad_conv,
        owned_out,
        owned_norm2,
        owned_gate_up,
        owned_down,
        new_norm1,
        new_in,
        new_conv,
        new_out,
        new_norm2,
        new_gate_up,
        new_down,
        new_first_norm1,
        new_first_in,
        new_first_conv,
        new_first_out,
        new_first_norm2,
        new_first_gate_up,
        new_first_down,
        new_second_norm1,
        new_second_in,
        new_second_conv,
        new_second_out,
        new_second_norm2,
        new_second_gate_up,
        new_second_down,
    )


def solution(mesh):
    n_dp, n_ctx, n_tp = (mesh.shape[name] for name in ("dp", "ctx", "tp"))
    n_lo = 2 if n_tp % 2 == 0 else 1
    devices = mesh.devices.reshape(n_dp, n_ctx, n_tp // n_lo, n_lo)
    paired = Mesh(devices, ("dp", "ctx", "hi", "lo"))
    tp = ("hi", "lo")

    row = P("dp", "ctx", None)
    params = (
        P(DATA),
        P(None, DATA, tp),
        P(None, tp),
        P(tp, DATA),
        P(DATA),
        P(None, DATA, tp),
        P(tp, DATA),
    )

    return jax.shard_map(
        per_device,
        mesh=paired,
        in_specs=(row, row, P("dp", None), *params, *params, *params),
        out_specs=(row, row, *params, *params, *params, *params),
        check_vma=False,
    )
```
